256 devices in a mesh: cells: 64 (over z, x, core), chan: 4 (over y).
Axes of the slice: x: 4, y: 4, z: 8, core: 2. Of those that a mesh axis runs over, the one named last changes fastest.
Arguments:
- charges: bfloat16 [128, 65536], P('chan', 'cells'), may hold values from -6 to 6
- basis: float32 [25, 65536], P(None, 'cells'), may hold values from -1.5 to 1.5
- atom_leaf: int32 [65536], P('cells'), may hold values from 0 to 8191, as said below
- leaf_lists: int32 [64, 8192], P(None, 'cells'), may hold values from -1 to 8191, as said below
- coarse_lists: int32 [64, 1024], P(None, 'cells'), may hold values from -1 to 1023, as said below
- up_ops: bfloat16 [8, 25, 25], replicated, may hold values from -0.4375 to 0.4375
- down_ops: bfloat16 [8, 25, 25], replicated, may hold values from -1.25 to 1.25
- leaf_ops: bfloat16 [25, 25, 64], replicated, may hold values from -0.15625 to 0.15625
- coarse_ops: bfloat16 [25, 25, 64], replicated, may hold values from -0.15625 to 0.15625
- mix: bfloat16 [128, 128], replicated, may hold values from -0.5 to 0.5
- cotangent: bfloat16 [128, 65536], P('chan', 'cells'), may hold values from -0.005859375 to 0.005859375
Outputs:
- refined: bfloat16 [128, 65536], P('chan', 'cells')
- grad_leaf_ops: float32 [25, 25, 64], replicated
- grad_coarse_ops: float32 [25, 25, 64], replicated
The draws below stay inside these ranges and needn't reach their ends.
Inputs may be any that keep to these rules, and one draw needn't show every extreme that they name: `atom_leaf`: an atom's leaf is one of the 128 consecutive leaves whose block along cells holds that atom. `leaf_lists`: entry [s, t] is -1 for an empty slot, else a leaf within 64 leaves of the block of 128 leaves that holds t. `coarse_lists`: entry [s, p] is -1 for an empty slot, else a parent cell within 8 cells of the block of 16 parent cells that holds p.
All inputs are finite; a program needn't handle non-finite values.
Results may differ from the reference program's by a relative error of at most 0.014.
Values may be sent and summed in bfloat16 or wider, within the bound.
A program may use at most 128 MiB of HBM per device.

```python
import jax
import jax.numpy as jnp
from jax import lax

C = 128
K = 25
SLOTS = 64
LEAF_DEV = 128
ATOMS_DEV = 1024
LEAVES = 8192
COARSE = 1024
ATOMS = 65536


def neighbour_lists(key, per_device, reach, overall):
    target = jnp.arange(overall, dtype=jnp.int32)[None, :]
    local_cell = target % per_device
    offset_cells = jax.random.randint(jax.random.fold_in(key, 11), (SLOTS, overall), -reach, reach + 1, dtype=jnp.int32)
    slot_index = jnp.arange(SLOTS, dtype=jnp.int32)[:, None]
    low_edge = (slot_index == 0) & (local_cell == 0)
    high_edge = (slot_index == 1) & (local_cell == per_device - 1)
    offset_cells = jnp.where(low_edge, -reach, jnp.where(high_edge, reach, offset_cells))
    partner = target + offset_cells
    dropped = jax.random.randint(jax.random.fold_in(key, 12), (SLOTS, overall), 0, 5, dtype=jnp.int32) == 0
    vacant = (dropped | (offset_cells == 0)) & jnp.logical_not(low_edge | high_edge)
    vacant = vacant | (partner < 0) | (partner >= overall)
    return jnp.where(vacant, -1, partner).astype(jnp.int32)


def draw_leaf_lists(key, part):
    return neighbour_lists(key, LEAF_DEV, LEAF_DEV // 2, LEAVES)


def draw_coarse_lists(key, part):
    return neighbour_lists(jax.random.fold_in(key, 5), LEAF_DEV // 8, LEAF_DEV // 16, COARSE)


def draw_atom_leaf(key, part):
    atom_index = jnp.arange(ATOMS, dtype=jnp.int32)
    device_of = atom_index // ATOMS_DEV
    within = atom_index % ATOMS_DEV
    first_draw = jax.random.randint(jax.random.fold_in(key, 21), (ATOMS,), 0, LEAF_DEV, dtype=jnp.int32)
    second_draw = jax.random.randint(jax.random.fold_in(key, 22), (ATOMS,), 1, LEAF_DEV + 1, dtype=jnp.int32)
    leaf_cell = first_draw * second_draw // LEAF_DEV
    leaf_cell = jnp.where(within == 0, LEAF_DEV - 1, jnp.where(within == 1, 0, leaf_cell))
    return (device_of * LEAF_DEV + leaf_cell).astype(jnp.int32)


def level_of(own_key, extent, split, low, largest):
    factor_of = 1.0
    for axis_at, blocks in split:
        steps = jax.random.uniform(jax.random.fold_in(jax.random.fold_in(own_key, 6), axis_at), (blocks,), jnp.float32, low / len(split), largest / len(split))
        factor_of = factor_of * jnp.repeat(jnp.exp(steps), extent[axis_at] // blocks).reshape((-1,) + (1,) * (len(extent) - 1 - axis_at))
    return factor_of


def centred(key, dims, deviation, most, cuts=(), kind=jnp.bfloat16):
    loudness = level_of(key, dims, cuts, -0.22, 0.18) if cuts else 1.0
    array = jax.random.normal(key, dims, jnp.float32) * deviation * loudness
    return jnp.minimum(jnp.maximum(array, -most), most).astype(kind)


def setup_inputs(seed: int = 0) -> dict:
    arg_keys = jax.random.split(jax.random.key(seed), 12)
    return {
        "charges": centred(arg_keys[0], (C, ATOMS), 1.0, 6.0, ((0, 4), (1, 64))),
        "basis": centred(arg_keys[1], (K, ATOMS), 0.25, 1.5, ((1, 64),), jnp.float32),
        "atom_leaf": draw_atom_leaf(jax.random.fold_in(arg_keys[11], 71), 0),
        "leaf_lists": draw_leaf_lists(jax.random.fold_in(arg_keys[11], 71), 0),
        "coarse_lists": draw_coarse_lists(jax.random.fold_in(arg_keys[11], 71), 0),
        "up_ops": centred(arg_keys[5], (8, K, K), (8 * K) ** -0.5, 0.4375),
        "down_ops": centred(arg_keys[6], (8, K, K), K ** -0.5, 1.25),
        "leaf_ops": centred(arg_keys[7], (K, K, SLOTS), (K * SLOTS) ** -0.5, 0.15625),
        "coarse_ops": centred(arg_keys[8], (K, K, SLOTS), (K * SLOTS) ** -0.5, 0.15625),
        "mix": centred(arg_keys[9], (C, C), C ** -0.5, 0.5),
        "cotangent": centred(arg_keys[10], (C, ATOMS), ((C * LEAVES) ** -0.5), 0.005859375, ((0, 4), (1, 64))),
    }


def to_leaves(weights, values, atom_leaf):
    def one_row(row):
        scaled = (row[None, :] * values).astype(jnp.bfloat16)
        scaled = lax.optimization_barrier(scaled).astype(jnp.float32)
        return jax.ops.segment_sum(scaled.T, atom_leaf, num_segments=LEAVES).T
    return lax.map(one_row, weights)


def from_leaves(weights, fields, atom_leaf):
    def advance(running, pieces):
        row, field = pieces
        return running + row[None, :] * jnp.take(field.astype(jnp.float32), atom_leaf, axis=1), None
    start_value = jnp.zeros((fields.shape[1], weights.shape[1]), jnp.float32)
    running, _ = lax.scan(advance, start_value, (weights, fields))
    return running


def pick(multipoles, slot_list):
    valid = slot_list >= 0
    picked = jnp.take(multipoles, jnp.where(valid, slot_list, 0).astype(jnp.int32), axis=2).astype(jnp.float32)
    return picked * valid.astype(jnp.float32)[None, None, :]


def translate(multipoles, lists, ops):
    slot_first = jnp.transpose(ops, (2, 0, 1))

    def advance(running, pieces):
        slot_list, slot_op = pieces
        picked = pick(multipoles, slot_list)
        return running + jnp.einsum("kj,jct->kct", slot_op.astype(jnp.float32), picked, precision=lax.Precision.HIGHEST), None
    start_value = jnp.zeros((multipoles.shape[0], multipoles.shape[1], lists.shape[1]), jnp.float32)
    running, _ = lax.scan(advance, start_value, (lists, slot_first))
    return running


def slot_gradients(multipoles, lists, fields):
    wide = fields.astype(jnp.float32)

    def one_slot(slot_list):
        return jnp.einsum("kct,jct->kj", wide, pick(multipoles, slot_list), precision=lax.Precision.HIGHEST)
    return jnp.transpose(lax.map(one_slot, lists), (1, 2, 0))


def reference(charges, basis, atom_leaf, leaf_lists, coarse_lists, up_ops, down_ops, leaf_ops, coarse_ops, mix, cotangent):
    highest = lax.Precision.HIGHEST
    moments = to_leaves(basis, charges.astype(jnp.float32), atom_leaf).astype(jnp.bfloat16)
    grouped = moments.astype(jnp.float32).reshape(K, C, COARSE, 8)
    coarse = jnp.einsum("okj,jcpo->kcp", up_ops.astype(jnp.float32), grouped, precision=highest).astype(jnp.bfloat16)
    near_field = translate(moments, leaf_lists, leaf_ops)
    far_field = translate(coarse, coarse_lists, coarse_ops).astype(jnp.bfloat16)
    child = jnp.einsum("okj,jcp->kcpo", down_ops.astype(jnp.float32), far_field.astype(jnp.float32), precision=highest)
    expansion = (near_field + child.reshape(K, C, LEAVES)).astype(jnp.bfloat16)
    potential = from_leaves(basis, expansion, atom_leaf).astype(jnp.bfloat16)
    mixed = jnp.dot(mix.T, potential, preferred_element_type=jnp.float32)
    refined = (charges.astype(jnp.float32) + mixed).astype(jnp.bfloat16)
    back_potential = jnp.dot(mix, cotangent, preferred_element_type=jnp.float32).astype(jnp.bfloat16)
    back_expansion = to_leaves(basis, back_potential.astype(jnp.float32), atom_leaf).astype(jnp.bfloat16)
    back_grouped = back_expansion.astype(jnp.float32).reshape(K, C, COARSE, 8)
    back_far = jnp.einsum("okj,kcpo->jcp", down_ops.astype(jnp.float32), back_grouped, precision=highest).astype(jnp.bfloat16)
    grad_leaf_ops = slot_gradients(moments, leaf_lists, back_expansion)
    grad_coarse_ops = slot_gradients(coarse, coarse_lists, back_far)
    return refined, grad_leaf_ops, grad_coarse_ops
```

```python
import functools

import jax
import jax.numpy as jnp
from jax import lax
from jax.experimental import pallas as pl
from jax.experimental.pallas import tpu as pltpu
from jax.sharding import PartitionSpec as P

MESH = pl.DeviceIdType.MESH
BF16 = jnp.bfloat16
F32 = jnp.float32
KP = 32
CH = 32
LD = 128
CD = 16
SG = 8
NN = (((1,), (0,)), ((), ()))
NT = (((1,), (1,)), ((), ()))


def dot(a, b, dims=NN):
    return lax.dot_general(a, b, dims, preferred_element_type=F32)


def one_hot(row, rows):
    index = lax.broadcasted_iota(jnp.int32, (rows, row.shape[1]), 0)
    return jnp.where(index == row, 1.0, 0.0).astype(BF16)


def lane_iota(rows, lanes):
    return lax.broadcasted_iota(jnp.int32, (rows, lanes), 1)


def fill_member(leaf_ref, member, first):
    member[...] = one_hot(leaf_ref[...] - first, LD)


def fill_basis(basis_ref, basis_pad):
    k = basis_ref.shape[0]
    basis_pad[...] = jnp.zeros_like(basis_pad)
    basis_pad[0:k, :] = basis_ref[...]


def fill_octants(octants):
    for o in range(8):
        lane = lane_iota(1, 128)
        row = (lane >> 4) * 128 + 8 * (lane & 15) + o
        octants[:, o * 128 : (o + 1) * 128] = one_hot(row, 1024)


def spread(values_ref, basis_pad, member, out):
    def block(b, carry):
        values = values_ref[pl.ds(pl.multiple_of(b * 16, 16), 16), :].astype(F32)
        for quad in range(4):
            scaled = jnp.concatenate(
                [
                    (basis_pad[...] * values[c : c + 1, :]).astype(BF16)
                    for c in range(quad * 4, quad * 4 + 4)
                ],
                axis=0,
            )
            row = pl.multiple_of(b * 512 + quad * 128, 128)
            out[pl.ds(row, 128), 0:LD] = dot(scaled, member[...], NT).astype(BF16)
        return carry

    lax.fori_loop(0, CH // 16, block, 0)


def to_parents(fields, octants, ops, stack):
    wide = jnp.concatenate(
        [
            jnp.concatenate(
                [fields[(cb * 8 + c) * KP : (cb * 8 + c + 1) * KP, 0:LD] for c in range(8)], axis=1
            )
            for cb in range(4)
        ],
        axis=0,
    )
    for o in range(8):
        part = dot(wide, octants[:, o * 128 : (o + 1) * 128]).astype(BF16)
        for cb in range(4):
            stack[o * KP : (o + 1) * KP, cb * 128 : (cb + 1) * 128] = part[cb * KP : (cb + 1) * KP]
    return dot(ops, stack[...]).astype(BF16)


def near_kernel(n_chan, cells_axis, *refs):
    (charges_ref, basis_ref, leaf_ref, up_ref, downt_ref, mix_ref, cot_ref) = refs[:7]
    (src_ref, csrc_ref, back_ref, bfar_ref) = refs[7:11]
    (cot_all, basis_pad, member, octants, stack, back_pot, bexp, to_left, to_right, from_right,
     from_left, coarse, coarse_right, coarse_left, sends, recvs) = refs[11:]
    n_cells = cells_axis
    cells = lax.axis_index("cells")
    chan = lax.axis_index("chan")
    left = lax.rem(cells + n_cells - 1, n_cells)
    right = lax.rem(cells + 1, n_cells)
    barrier = pltpu.get_barrier_semaphore()
    for r in range(1, n_chan):
        pl.semaphore_signal(
            barrier, inc=1, device_id=(cells, lax.rem(chan + r, n_chan)), device_id_type=MESH
        )
    for side in (left, right):
        pl.semaphore_signal(barrier, inc=1, device_id=(side, chan), device_id_type=MESH)
    pl.semaphore_wait(barrier, n_chan + 1)

    mine = pl.ds(pl.multiple_of(chan * CH, CH), CH)
    copies = []
    for r in range(1, n_chan):
        copy = pltpu.make_async_remote_copy(
            src_ref=cot_ref,
            dst_ref=cot_all.at[mine, :],
            send_sem=sends.at[r],
            recv_sem=recvs.at[r],
            device_id=(cells, lax.rem(chan + r, n_chan)),
            device_id_type=MESH,
        )
        copy.start()
        copies.append(copy)

    fill_member(leaf_ref, member, cells * LD)
    fill_basis(basis_ref, basis_pad)
    spread(charges_ref, basis_pad, member, src_ref)
    low = lane_iota(512, 128) < 64
    top = src_ref[0:512, 0:LD].astype(F32)
    bottom = pltpu.roll(src_ref[512:1024, 0:LD].astype(F32), 64, 1)
    to_left[...] = jnp.where(low, top, bottom).astype(BF16)
    to_right[...] = jnp.where(low, bottom, top).astype(BF16)
    halo = []
    for i, (source, target, side) in enumerate(
        ((to_left, from_right, left), (to_right, from_left, right))
    ):
        copy = pltpu.make_async_remote_copy(
            src_ref=source,
            dst_ref=target,
            send_sem=sends.at[n_chan + i],
            recv_sem=recvs.at[n_chan + i],
            device_id=(side, chan),
            device_id_type=MESH,
        )
        copy.start()
        halo.append(copy)

    fill_octants(octants)
    coarse[...] = to_parents(src_ref, octants, up_ref[...], stack)
    for i, (target, side) in enumerate(((coarse_right, left), (coarse_left, right))):
        copy = pltpu.make_async_remote_copy(
            src_ref=coarse,
            dst_ref=target,
            send_sem=sends.at[n_chan + 2 + i],
            recv_sem=recvs.at[n_chan + 2 + i],
            device_id=(side, chan),
            device_id_type=MESH,
        )
        copy.start()
        halo.append(copy)

    cot_all[mine, :] = cot_ref[...]
    for copy in copies:
        copy.wait()
    back_pot[...] = dot(mix_ref[mine, :], cot_all[...]).astype(BF16)
    spread(back_pot, basis_pad, member, bexp)
    bfar_ref[...] = to_parents(bexp, octants, downt_ref[...], stack)
    for c in range(CH):
        back_ref[:, c * LD : (c + 1) * LD] = bexp[c * KP : (c + 1) * KP, :]

    for copy in halo:
        copy.wait()
    a, b = from_right[...].astype(F32), from_left[...].astype(F32)
    src_ref[0:512, LD : 2 * LD] = jnp.where(low, a, b).astype(BF16)
    src_ref[512:1024, LD : 2 * LD] = pltpu.roll(jnp.where(low, b, a), 64, 1).astype(BF16)
    first = (lane_iota(KP, 128) & 15) < 8
    for cb in range(4):
        lanes = slice(cb * 128, (cb + 1) * 128)
        rows = slice(cb * KP, (cb + 1) * KP)
        csrc_ref[rows, 0:128] = coarse[:, lanes]
        csrc_ref[rows, 128:256] = jnp.where(
            first, coarse_right[:, lanes].astype(F32), coarse_left[:, lanes].astype(F32)
        ).astype(BF16)


def gather_group(lists, group, source, picked):
    rows = lists[pl.ds(pl.multiple_of(group * SG, SG), SG), :]
    blocks = source.shape[0] // KP
    for pair in range(SG // 2):
        hot = jnp.concatenate(
            [one_hot(rows[s : s + 1, :], 256) for s in (2 * pair, 2 * pair + 1)], axis=1
        )
        for part in range(0, blocks, 4):
            got = dot(source[part * KP : (part + 4) * KP, :], hot).astype(BF16)
            for half in range(2):
                s = 2 * pair + half
                for i in range(4):
                    c = part + i
                    picked[s * KP : (s + 1) * KP, c * 128 : (c + 1) * 128] = got[
                        i * KP : (i + 1) * KP, half * 128 : (half + 1) * 128
                    ]


def field_kernel(*refs):
    (src_ref, csrc_ref, back_ref, bfar_ref, lists_ref, clists_ref, lops_ref, cops_ref, down_ref,
     basis_ref, leaf_ref) = refs[:11]
    (pot_ref, grad_ref) = refs[11:13]
    (lists, clists, picked, cpicked, near, far, slots, expand, basis_pad, member, pot) = refs[13:]
    cells = lax.axis_index("cells")
    n_slots = lists_ref.shape[0]
    groups = n_slots // SG
    k = basis_ref.shape[0]

    raw = lists_ref[...]
    lists[...] = jnp.where(raw < 0, -1, (raw - cells * LD) & 255)
    raw = clists_ref[...]
    at = jnp.where(raw < 0, -1, (raw - cells * CD) & 31)
    c8 = (lane_iota(n_slots, 128) >> 4) * CD
    clists[...] = jnp.where(at < 0, -1, jnp.where(at < CD, c8 + at, 112 + c8 + at))

    far[...] = jnp.zeros_like(far)

    def coarse_group(g, carry):
        gather_group(clists, g, csrc_ref, cpicked)
        ops = cops_ref[:, pl.ds(pl.multiple_of(g * 256, 256), 256)]
        far[...] += dot(ops, cpicked[...])
        row = pl.multiple_of((groups + g) * 256, 256)
        slots[pl.ds(row, 256), 0:KP] = dot(cpicked[...], bfar_ref[...], NT)
        return carry

    lax.fori_loop(0, groups, coarse_group, 0)

    far16 = far[...].astype(BF16)
    far_rows = jnp.concatenate([far16[:, cb * 128 : (cb + 1) * 128] for cb in range(4)], axis=0)
    octant = lane_iota(KP, 128) & 7
    for c in range(8):
        parent = (lane_iota(1, 128) >> 3) + c * CD
        wide = dot(far_rows, one_hot(parent, 128))
        for cb in range(4):
            lanes = slice((cb * 8 + c) * 128, (cb * 8 + c + 1) * 128)
            block = wide[cb * KP : (cb + 1) * KP, :]
            for o in range(8):
                picked[o * KP : (o + 1) * KP, lanes] = jnp.where(octant == o, block, 0.0).astype(BF16)
    for c in range(0, CH * LD, 512):
        near[:, c : c + 512] = dot(down_ref[...], picked[:, c : c + 512])

    def leaf_group(g, carry):
        gather_group(lists, g, src_ref, picked)
        ops = lops_ref[:, pl.ds(pl.multiple_of(g * 256, 256), 256)]
        for c in range(0, CH * LD, 512):
            near[:, c : c + 512] += dot(ops, picked[:, c : c + 512])
        row = pl.multiple_of(g * 256, 256)
        slots[pl.ds(row, 256), 0:KP] = dot(picked[...], back_ref[...], NT)
        return carry

    lax.fori_loop(0, groups, leaf_group, 0)

    for c in range(CH):
        expand[c * KP : (c + 1) * KP, :] = near[:, c * LD : (c + 1) * LD].astype(BF16)
    fill_member(leaf_ref, member, cells * LD)
    fill_basis(basis_ref, basis_pad)

    def collect(b, carry):
        rows = []
        for quad in range(4):
            row = pl.multiple_of(b * 512 + quad * 128, 128)
            per_atom = dot(expand[pl.ds(row, 128), :], member[...])
            for c in range(4):
                rows.append(
                    jnp.sum(
                        per_atom[c * KP : (c + 1) * KP, :] * basis_pad[...], axis=0, keepdims=True
                    )
                )
        pot_ref[pl.ds(pl.multiple_of(b * 16, 16), 16), :] = jnp.concatenate(rows, axis=0).astype(BF16)
        return carry

    lax.fori_loop(0, CH // 16, collect, 0)

    grad_ref[...] = jnp.zeros_like(grad_ref)
    for j in range(k):
        turned = slots[pl.ds(j, 2 * n_slots, stride=KP), :].T
        for i in range(k):
            grad_ref[i * k + j : i * k + j + 1, :] = turned[i : i + 1, :]


def mix_kernel(n_chan, n_x, n_z, k, rc, *refs):
    (pot_ref, grad_ref, charges_ref, mix_ref) = refs[:4]
    (out_ref, gl_ref, gc_ref) = refs[4:7]
    (pot_all, mixt, half_in, half, part_in, part, plane_in, total, send_p, recv_p, send_h, recv_h, send_x,
     recv_x, send_z, recv_z, send_g, recv_g, send_e, recv_e) = refs[7:]
    cells = lax.axis_index("cells")
    chan = lax.axis_index("chan")
    core = lax.rem(cells, 2)
    x = lax.rem(cells // 2, n_x)
    z = cells // (2 * n_x)
    n_plane = n_x * n_chan
    m = x * n_chan + chan
    slots = gl_ref.shape[2]

    other = (cells + 1 - 2 * core, chan)

    def plane_peer(r):
        d = lax.rem(m + r, n_plane)
        return d, ((z * n_x + d // n_chan) * 2 + core, lax.rem(d, n_chan))

    def z_peer(r):
        d = lax.rem(z + r, n_z)
        return d, ((d * n_x + x) * 2 + core, chan)

    barrier = pltpu.get_barrier_semaphore()
    pl.semaphore_signal(barrier, inc=1, device_id=other, device_id_type=MESH)
    for r in range(1, n_plane):
        pl.semaphore_signal(barrier, inc=1, device_id=plane_peer(r)[1], device_id_type=MESH)
    for r in range(1, n_z):
        pl.semaphore_signal(barrier, inc=1, device_id=z_peer(r)[1], device_id_type=MESH)
    pl.semaphore_wait(barrier, n_plane + n_z - 1)

    size = n_plane * rc
    half_copy = pltpu.make_async_remote_copy(
        src_ref=grad_ref.at[pl.ds(pl.multiple_of((1 - core) * size, 8), size), :],
        dst_ref=half_in,
        send_sem=send_h,
        recv_sem=recv_h,
        device_id=other,
        device_id_type=MESH,
    )
    half_copy.start()
    mine = pl.ds(pl.multiple_of(chan * CH, CH), CH)
    pot_copies = []
    for r in range(1, n_chan):
        copy = pltpu.make_async_remote_copy(
            src_ref=pot_ref,
            dst_ref=pot_all.at[mine, :],
            send_sem=send_p.at[r],
            recv_sem=recv_p.at[r],
            device_id=(cells, lax.rem(chan + r, n_chan)),
            device_id_type=MESH,
        )
        copy.start()
        pot_copies.append(copy)
    pot_all[mine, :] = pot_ref[...]
    mixt[...] = mix_ref[...].astype(F32).T.astype(BF16)

    half_copy.wait()
    half[...] = grad_ref[pl.ds(pl.multiple_of(core * size, 8), size), :] + half_in[...]

    def exchange(source_of, target, peers, send, recv):
        copies = []
        for r, (d, device) in peers:
            copy = pltpu.make_async_remote_copy(
                src_ref=source_of(d),
                dst_ref=target(r),
                send_sem=send.at[r],
                recv_sem=recv.at[r],
                device_id=device,
                device_id_type=MESH,
            )
            copy.start()
            copies.append(copy)
        return copies

    def rows(d):
        return pl.ds(pl.multiple_of(d * rc, 8), rc)

    plane = [(r, plane_peer(r)) for r in range(1, n_plane)]
    copies = exchange(lambda d: half.at[rows(d), :], lambda r: part_in.at[r], plane, send_x, recv_x)
    for copy in pot_copies:
        copy.wait()
    out_ref[...] = (
        charges_ref[...].astype(F32) + dot(mixt[mine, :], pot_all[...])
    ).astype(BF16)
    for copy in copies:
        copy.wait()
    summed = half[rows(m), :]
    for r in range(1, n_plane):
        summed = summed + part_in[r]
    part[...] = summed

    copies = exchange(
        lambda d: part, lambda r: plane_in.at[z], [(r, z_peer(r)) for r in range(1, n_z)], send_z, recv_z
    )
    plane_in[z] = part[...]
    for copy in copies:
        copy.wait()
    summed = plane_in[0]
    for r in range(1, n_z):
        summed = summed + plane_in[r]
    first = core * size
    own = pl.ds(pl.multiple_of(first + m * rc, 8), rc)
    total[own, :] = summed

    copies = exchange(lambda d: total.at[own, :], lambda r: total.at[own, :], plane, send_g, recv_g)
    for copy in copies:
        copy.wait()
    side = pl.ds(pl.multiple_of(first, 8), size)
    last = pltpu.make_async_remote_copy(
        src_ref=total.at[side, :],
        dst_ref=total.at[side, :],
        send_sem=send_e,
        recv_sem=recv_e,
        device_id=other,
        device_id_type=MESH,
    )
    last.start()
    last.wait()
    for i in range(k):
        block = total[i * k : (i + 1) * k, :]
        gl_ref[i] = block[:, 0:slots]
        gc_ref[i] = pltpu.roll(block, 128 - slots, 1)[:, 0:slots]


def ops_rows(ops, pad_out):
    k, _, s = ops.shape
    turned = jnp.pad(jnp.transpose(ops, (0, 2, 1)), ((0, KP - k), (0, 0), (0, KP - k)))
    return turned.reshape(KP, s * KP)


def octant_rows(ops):
    o, k, _ = ops.shape
    return jnp.pad(jnp.transpose(ops, (1, 0, 2)), ((0, KP - k), (0, 0), (0, KP - k))).reshape(KP, o * KP)


VMEM = pl.BlockSpec(memory_space=pltpu.VMEM)


def call(kernel, outs, scratch, args, collective=None):
    extra = {}
    if collective is not None:
        extra = dict(collective_id=collective, has_side_effects=True)
    return pl.pallas_call(
        kernel,
        out_shape=outs,
        in_specs=[VMEM] * len(args),
        out_specs=[VMEM] * len(outs),
        scratch_shapes=scratch,
        compiler_params=pltpu.CompilerParams(vmem_limit_bytes=60 << 20, **extra),
    )(*args)


def local(n_cells, n_chan, n_x, n_z, charges, basis, atom_leaf, leaf_lists, coarse_lists, up_ops, down_ops, leaf_ops,
          coarse_ops, mix, cotangent):
    k, atoms = basis.shape
    slots = leaf_lists.shape[0]
    shape = jax.ShapeDtypeStruct
    dma = pltpu.SemaphoreType.DMA
    leaf_row = atom_leaf.reshape(1, atoms)
    n_plane = n_x * n_chan
    rc = -(-k * k // (16 * n_plane)) * 8

    src, csrc, back, bfar = call(
        functools.partial(near_kernel, n_chan, n_cells),
        [
            shape((CH * KP, 2 * LD), BF16),
            shape((4 * KP, 256), BF16),
            shape((KP, CH * LD), BF16),
            shape((KP, CH * CD), BF16),
        ],
        [
            pltpu.VMEM((n_chan * CH, atoms), BF16),
            pltpu.VMEM((KP, atoms), F32),
            pltpu.VMEM((LD, atoms), BF16),
            pltpu.VMEM((1024, 1024), BF16),
            pltpu.VMEM((8 * KP, CH * CD), BF16),
            pltpu.VMEM((CH, atoms), BF16),
            pltpu.VMEM((CH * KP, LD), BF16),
            pltpu.VMEM((512, LD), BF16),
            pltpu.VMEM((512, LD), BF16),
            pltpu.VMEM((512, LD), BF16),
            pltpu.VMEM((512, LD), BF16),
            pltpu.VMEM((KP, CH * CD), BF16),
            pltpu.VMEM((KP, CH * CD), BF16),
            pltpu.VMEM((KP, CH * CD), BF16),
            dma((n_chan + 4,)),
            dma((n_chan + 4,)),
        ],
        (charges, basis, leaf_row, octant_rows(up_ops), octant_rows(jnp.transpose(down_ops, (0, 2, 1))), mix,
         cotangent),
        collective=0,
    )

    pot, grads = call(
        field_kernel,
        [shape((CH, atoms), BF16), shape((2 * n_plane * rc, 128), F32)],
        [
            pltpu.VMEM((slots, LD), jnp.int32),
            pltpu.VMEM((slots, 128), jnp.int32),
            pltpu.VMEM((SG * KP, CH * LD), BF16),
            pltpu.VMEM((SG * KP, CH * CD), BF16),
            pltpu.VMEM((KP, CH * LD), F32),
            pltpu.VMEM((KP, CH * CD), F32),
            pltpu.VMEM((2 * slots * KP, 128), F32),
            pltpu.VMEM((CH * KP, LD), BF16),
            pltpu.VMEM((KP, atoms), F32),
            pltpu.VMEM((LD, atoms), BF16),
            pltpu.VMEM((CH, atoms), F32),
        ],
        (src, csrc, back, bfar, leaf_lists, jnp.tile(coarse_lists, (1, 8)), ops_rows(leaf_ops, KP),
         ops_rows(coarse_ops, KP), octant_rows(down_ops), basis, leaf_row),
    )

    refined, gl, gc = call(
        functools.partial(mix_kernel, n_chan, n_x, n_z, k, rc),
        [shape((CH, atoms), BF16), shape((k, k, slots), F32), shape((k, k, slots), F32)],
        [
            pltpu.VMEM((n_chan * CH, atoms), BF16),
            pltpu.VMEM(mix.shape, BF16),
            pltpu.VMEM((n_plane * rc, 128), F32),
            pltpu.VMEM((n_plane * rc, 128), F32),
            pltpu.VMEM((n_plane, rc, 128), F32),
            pltpu.VMEM((rc, 128), F32),
            pltpu.VMEM((n_z, rc, 128), F32),
            pltpu.VMEM((2 * n_plane * rc, 128), F32),
            dma((n_chan,)),
            dma((n_chan,)),
            dma,
            dma,
            dma((n_plane,)),
            dma((n_plane,)),
            dma((n_z,)),
            dma((n_z,)),
            dma((n_plane,)),
            dma((n_plane,)),
            dma,
            dma,
        ],
        (pot, grads, charges, mix),
        collective=1,
    )
    return refined, gl, gc


def solution(mesh):
    n_cells, n_chan = mesh.shape["cells"], mesh.shape["chan"]
    n_x = 4 if n_cells % 8 == 0 and n_cells > 8 else 2
    n_z = n_cells // (2 * n_x)
    placed = (
        P("chan", "cells"),
        P(None, "cells"),
        P("cells"),
        P(None, "cells"),
        P(None, "cells"),
        P(),
        P(),
        P(),
        P(),
        P(),
        P("chan", "cells"),
    )
    return jax.shard_map(
        functools.partial(local, n_cells, n_chan, n_x, n_z),
        mesh=mesh,
        in_specs=placed,
        out_specs=(P("chan", "cells"), P(), P()),
        check_vma=False,
    )
```

```python
import functools

import jax
import jax.numpy as jnp
from jax import lax
from jax.experimental import pallas as pl
from jax.experimental.pallas import tpu as pltpu
from jax.sharding import PartitionSpec as P

MESH = pl.DeviceIdType.MESH
BF16 = jnp.bfloat16
F32 = jnp.float32
KP = 32
CH = 32
LD = 128
CD = 16
SG = 8
NN = (((1,), (0,)), ((), ()))
NT = (((1,), (1,)), ((), ()))
TN = (((0,), (0,)), ((), ()))


def dot(a, b, dims=NN):
    return lax.dot_general(a, b, dims, preferred_element_type=F32)


def one_hot(row, rows):
    index = lax.broadcasted_iota(jnp.int32, (rows, row.shape[1]), 0)
    return jnp.where(index == row, 1.0, 0.0).astype(BF16)


def lane_iota(rows, lanes):
    return lax.broadcasted_iota(jnp.int32, (rows, lanes), 1)


def fill_member(leaf_ref, member, first):
    member[...] = one_hot(leaf_ref[...] - first, LD)


def fill_basis(basis_ref, basis_pad):
    k = basis_ref.shape[0]
    basis_pad[...] = jnp.zeros_like(basis_pad)
    basis_pad[0:k, :] = basis_ref[...]


def fill_octants(octants):
    for o in range(8):
        lane = lane_iota(1, 128)
        row = (lane >> 4) * 128 + 8 * (lane & 15) + o
        octants[:, o * 128 : (o + 1) * 128] = one_hot(row, 1024)


def spread(values_ref, basis_pad, member, out):
    def block(b, carry):
        values = values_ref[pl.ds(pl.multiple_of(b * 16, 16), 16), :].astype(F32)
        for quad in range(4):
            scaled = jnp.concatenate(
                [
                    (basis_pad[...] * values[c : c + 1, :]).astype(BF16)
                    for c in range(quad * 4, quad * 4 + 4)
                ],
                axis=0,
            )
            row = pl.multiple_of(b * 512 + quad * 128, 128)
            out[pl.ds(row, 128), 0:LD] = dot(scaled, member[...], NT).astype(BF16)
        return carry

    lax.fori_loop(0, CH // 16, block, 0)


def to_parents(fields, octants, ops, dims, stack):
    wide = jnp.concatenate(
        [
            jnp.concatenate(
                [fields[(cb * 8 + c) * KP : (cb * 8 + c + 1) * KP, 0:LD] for c in range(8)], axis=1
            )
            for cb in range(4)
        ],
        axis=0,
    )
    for o in range(8):
        part = dot(wide, octants[:, o * 128 : (o + 1) * 128]).astype(BF16)
        for cb in range(4):
            stack[o * KP : (o + 1) * KP, cb * 128 : (cb + 1) * 128] = part[cb * KP : (cb + 1) * KP]
    return dot(ops, stack[...], dims).astype(BF16)


def gather_group(lists, group, source, picked, base):
    rows = lists[pl.ds(pl.multiple_of(group * SG, SG), SG), :]
    blocks = source.shape[0] // KP
    for pair in range(SG // 2):
        hot = jnp.concatenate(
            [one_hot(rows[s : s + 1, :], 256) for s in (2 * pair, 2 * pair + 1)], axis=1
        )
        for part in range(0, blocks, 4):
            got = dot(source[part * KP : (part + 4) * KP, :], hot).astype(BF16)
            for half in range(2):
                s = 2 * pair + half
                for i in range(4):
                    c = part + i
                    picked[pl.ds(base + s * KP, KP), c * 128 : (c + 1) * 128] = got[
                        i * KP : (i + 1) * KP, half * 128 : (half + 1) * 128
                    ]


def group_rows(g):
    return pl.ds(pl.multiple_of(g * SG * KP, SG * KP), SG * KP)


def turn_ops(leaf_ops_ref, coarse_ops_ref, rows, turned, ops):
    k, _, s = leaf_ops_ref.shape
    rows[...] = jnp.zeros_like(rows)
    turned[...] = jnp.zeros_like(turned)
    for i in range(k):
        both = jnp.concatenate([leaf_ops_ref[i].astype(F32), coarse_ops_ref[i].astype(F32)], axis=1)
        rows[i * KP : i * KP + k, :] = both
    for j in range(k):
        turned[pl.ds(j, 2 * s, stride=KP), 0:KP] = rows[pl.ds(j, KP, stride=KP), :].T
    ops[...] = turned[:, 0:KP].astype(BF16)


def main_kernel(n_cells, n_chan, n_x, n_z, rc, names, *refs):
    r = dict(zip(names, refs))
    cells = lax.axis_index("cells")
    chan = lax.axis_index("chan")
    core = lax.rem(cells, 2)
    x = lax.rem(cells // 2, n_x)
    z = cells // (2 * n_x)
    n_plane = n_x * n_chan
    m = x * n_chan + chan
    k = r["basis"].shape[0]
    n_slots = r["leaf_lists"].shape[0]
    groups = n_slots // SG
    left = (lax.rem(cells + n_cells - 1, n_cells), chan)
    right = (lax.rem(cells + 1, n_cells), chan)
    other = (cells + 1 - 2 * core, chan)
    chan_peers = [(cells, lax.rem(chan + i, n_chan)) for i in range(1, n_chan)]
    plane_peers, z_peers = [], []
    for i in range(1, n_plane):
        d = lax.rem(m + i, n_plane)
        plane_peers.append((d, ((z * n_x + d // n_chan) * 2 + core, lax.rem(d, n_chan))))
    for i in range(1, n_z):
        d = lax.rem(z + i, n_z)
        z_peers.append((d, ((d * n_x + x) * 2 + core, chan)))

    barrier = pltpu.get_barrier_semaphore()
    greeted = chan_peers + [left, right, other] + [d for _, d in plane_peers] + [d for _, d in z_peers]
    for device in greeted:
        pl.semaphore_signal(barrier, inc=1, device_id=device, device_id_type=MESH)

    sems = {"next": 0}

    def send(source, target, device):
        i = sems["next"]
        sems["next"] = i + 1
        copy = pltpu.make_async_remote_copy(
            src_ref=source,
            dst_ref=target,
            send_sem=r["sends"].at[i],
            recv_sem=r["recvs"].at[i],
            device_id=device,
            device_id_type=MESH,
        )
        copy.start()
        return copy

    member, basis_pad, src, bexp = r["member"], r["basis_pad"], r["src"], r["bexp"]
    fill_member(r["leaf"], member, cells * LD)
    fill_basis(r["basis"], basis_pad)
    pl.semaphore_wait(barrier, len(greeted))

    mine = pl.ds(pl.multiple_of(chan * CH, CH), CH)
    cot_copies = [send(r["cot"], r["cot_all"].at[mine, :], d) for d in chan_peers]

    spread(r["charges"], basis_pad, member, src)
    low = lane_iota(512, 128) < 64
    top = src[0:512, 0:LD].astype(F32)
    bottom = pltpu.roll(src[512:1024, 0:LD].astype(F32), 64, 1)
    r["to_left"][...] = jnp.where(low, top, bottom).astype(BF16)
    r["to_right"][...] = jnp.where(low, bottom, top).astype(BF16)
    halo = [send(r["to_left"], r["from_right"], left), send(r["to_right"], r["from_left"], right)]

    for ops_ref, pad in ((r["up"], r["up_pad"]), (r["down"], r["down_pad"])):
        pad[...] = jnp.zeros_like(pad)
        for o in range(8):
            pad[o * KP : o * KP + k, 0:k] = ops_ref[o].astype(F32)
    fill_octants(r["octants"])

    up_wide = jnp.concatenate([r["up_pad"][o * KP : (o + 1) * KP, :] for o in range(8)], axis=1).astype(BF16)
    down_wide = jnp.concatenate([r["down_pad"][o * KP : (o + 1) * KP, :] for o in range(8)], axis=1).astype(BF16)
    down_tall = r["down_pad"][...].astype(BF16)

    coarse = r["coarse"]
    coarse[...] = to_parents(src, r["octants"], up_wide, NN, r["stack"])
    coarse_halo = [send(coarse, r["coarse_right"], left), send(coarse, r["coarse_left"], right)]

    turn_ops(r["leaf_ops"], r["coarse_ops"], r["total"], r["slots"], r["ops"])

    raw = r["leaf_lists"][...]
    r["lists"][...] = jnp.where(raw < 0, -1, (raw - cells * LD) & 255)
    raw = r["coarse_lists"][...]
    raw = jnp.concatenate([raw] * 8, axis=1)
    at = jnp.where(raw < 0, -1, (raw - cells * CD) & 31)
    c8 = (lane_iota(n_slots, 128) >> 4) * CD
    r["clists"][...] = jnp.where(at < 0, -1, jnp.where(at < CD, c8 + at, 112 + c8 + at))

    r["cot_all"][mine, :] = r["cot"][...]
    for copy in cot_copies:
        copy.wait()
    r["back_pot"][...] = dot(r["mix"][mine, :], r["cot_all"][...]).astype(BF16)
    spread(r["back_pot"], basis_pad, member, bexp)
    r["bfar"][...] = to_parents(bexp, r["octants"], down_tall, TN, r["stack"])
    for c in range(CH):
        r["back"][:, c * LD : (c + 1) * LD] = bexp[c * KP : (c + 1) * KP, :]

    for copy in coarse_halo:
        copy.wait()
    first = (lane_iota(KP, 128) & 15) < 8
    csrc = r["csrc"]
    for cb in range(4):
        lanes = slice(cb * 128, (cb + 1) * 128)
        rows = slice(cb * KP, (cb + 1) * KP)
        csrc[rows, 0:128] = coarse[:, lanes]
        csrc[rows, 128:256] = jnp.where(
            first, r["coarse_right"][:, lanes].astype(F32), r["coarse_left"][:, lanes].astype(F32)
        ).astype(BF16)

    picked, cpicked, slots = r["picked"], r["cpicked"], r["slots"]

    def coarse_group(g, carry):
        base = pl.multiple_of(g * SG * KP, SG * KP)
        gather_group(r["clists"], g, csrc, cpicked, base)
        slots[group_rows(groups + g), 0:KP] = dot(cpicked[group_rows(g), :], r["bfar"][...], NT)
        return carry

    lax.fori_loop(0, groups, coarse_group, 0)

    for copy in halo:
        copy.wait()
    a, b = r["from_right"][...].astype(F32), r["from_left"][...].astype(F32)
    src[0:512, LD : 2 * LD] = jnp.where(low, a, b).astype(BF16)
    src[512:1024, LD : 2 * LD] = pltpu.roll(jnp.where(low, b, a), 64, 1).astype(BF16)

    def leaf_group(g, carry):
        base = pl.multiple_of(g * SG * KP, SG * KP)
        gather_group(r["lists"], g, src, picked, base)
        slots[group_rows(g), 0:KP] = dot(picked[group_rows(g), :], r["back"][...], NT)
        return carry

    lax.fori_loop(0, groups, leaf_group, 0)

    grad = r["grad"]
    size = n_plane * rc
    grad[2 * size - 8 * ((2 * size - k * k) // 8) - 8 :, :] = jnp.zeros(
        (8 * ((2 * size - k * k) // 8) + 8, 128), F32
    )
    for j in range(k):
        turned = slots[pl.ds(j, 2 * n_slots, stride=KP), :].T
        grad[pl.ds(j, k, stride=k), :] = turned[0:k, :]
    half_copy = send(
        grad.at[pl.ds(pl.multiple_of((1 - core) * size, 8), size), :], r["half_in"], other
    )

    near, far = r["near"], r["far"]
    far[...] = jnp.zeros_like(far)

    def far_group(g, carry):
        far[...] += dot(r["ops"][group_rows(groups + g), :], cpicked[group_rows(g), :], TN)
        return carry

    lax.fori_loop(0, groups, far_group, 0)
    half_copy.wait()
    half = r["half"]
    half[...] = grad[pl.ds(pl.multiple_of(core * size, 8), size), :] + r["half_in"][...]

    def chunk(d):
        return pl.ds(pl.multiple_of(d * rc, 8), rc)

    plane_copies = [
        send(half.at[chunk(d), :], r["part_in"].at[i], device)
        for i, (d, device) in enumerate(plane_peers)
    ]

    far16 = far[...].astype(BF16)
    far_rows = jnp.concatenate([far16[:, cb * 128 : (cb + 1) * 128] for cb in range(4)], axis=0)
    octant = lane_iota(KP, 128) & 7
    child = r["child"]
    for c in range(8):
        parent = (lane_iota(1, 128) >> 3) + c * CD
        wide = dot(far_rows, one_hot(parent, 128))
        for cb in range(4):
            lanes = slice((cb * 8 + c) * 128, (cb * 8 + c + 1) * 128)
            block = wide[cb * KP : (cb + 1) * KP, :]
            for o in range(8):
                child[o * KP : (o + 1) * KP, lanes] = jnp.where(octant == o, block, 0.0).astype(BF16)
    for c in range(0, CH * LD, 512):
        near[:, c : c + 512] = dot(down_wide, child[:, c : c + 512])

    def near_group(g, carry):
        ops = r["ops"][group_rows(g), :]
        for c in range(0, CH * LD, 512):
            near[:, c : c + 512] += dot(ops, picked[group_rows(g), c : c + 512], TN)
        return carry

    lax.fori_loop(0, groups // 2, near_group, 0)

    for copy in plane_copies:
        copy.wait()
    summed = half[chunk(m), :]
    for i in range(n_plane - 1):
        summed = summed + r["part_in"][i]
    r["part"][...] = summed
    z_copies = [send(r["part"], r["z_in"].at[z], device) for _, device in z_peers]
    r["z_in"][z] = summed

    lax.fori_loop(groups // 2, groups, near_group, 0)

    for copy in z_copies:
        copy.wait()
    summed = r["z_in"][0]
    for i in range(1, n_z):
        summed = summed + r["z_in"][i]
    total = r["total_out"]
    own = pl.ds(pl.multiple_of(core * size + m * rc, 8), rc)
    total[own, :] = summed
    gather_copies = [send(total.at[own, :], total.at[own, :], device) for _, device in plane_peers]

    expand = bexp
    for c in range(CH):
        expand[c * KP : (c + 1) * KP, :] = near[:, c * LD : (c + 1) * LD].astype(BF16)

    def collect(b, carry):
        rows = []
        for quad in range(4):
            row = pl.multiple_of(b * 512 + quad * 128, 128)
            per_atom = dot(expand[pl.ds(row, 128), :], member[...])
            for c in range(4):
                rows.append(
                    jnp.sum(
                        per_atom[c * KP : (c + 1) * KP, :] * basis_pad[...], axis=0, keepdims=True
                    )
                )
        pot[pl.ds(pl.multiple_of(b * 16, 16), 16), :] = jnp.concatenate(rows, axis=0).astype(BF16)
        return carry

    pot = r["pot"]
    lax.fori_loop(0, CH // 16, collect, 0)
    pot_all = r["pot_all"]
    pot_copies = [send(pot, pot_all.at[mine, :], d) for d in chan_peers]
    pot_all[mine, :] = pot[...]

    for copy in gather_copies:
        copy.wait()
    side = pl.ds(pl.multiple_of(core * size, 8), size)
    last = send(total.at[side, :], total.at[side, :], other)
    for copy in pot_copies:
        copy.wait()
    last.wait()


def final_kernel(pot_ref, total_ref, charges_ref, mix_ref, out_ref, gl_ref, gc_ref, mixt):
    chan = lax.axis_index("chan")
    k, _, slots = gl_ref.shape
    mixt[...] = mix_ref[...].astype(F32).T.astype(BF16)
    mine = pl.ds(pl.multiple_of(chan * CH, CH), CH)
    out_ref[...] = (charges_ref[...].astype(F32) + dot(mixt[mine, :], pot_ref[...])).astype(BF16)
    for i in range(k):
        block = total_ref[i * k : (i + 1) * k, :]
        gl_ref[i] = block[:, 0:slots]
        gc_ref[i] = pltpu.roll(block, 128 - slots, 1)[:, 0:slots]


VMEM = pl.BlockSpec(memory_space=pltpu.VMEM)


def call(kernel, outs, scratch, args, collective=None):
    extra = {}
    if collective is not None:
        extra = dict(collective_id=collective, has_side_effects=True)
    return pl.pallas_call(
        kernel,
        out_shape=outs,
        in_specs=[VMEM] * len(args),
        out_specs=[VMEM] * len(outs),
        scratch_shapes=scratch,
        compiler_params=pltpu.CompilerParams(vmem_limit_bytes=60 << 20, **extra),
    )(*args)


def local(n_cells, n_chan, n_x, n_z, charges, basis, atom_leaf, leaf_lists, coarse_lists, up_ops, down_ops, leaf_ops,
          coarse_ops, mix, cotangent):
    k, atoms = basis.shape
    slots = leaf_lists.shape[0]
    shape = jax.ShapeDtypeStruct
    n_plane = n_x * n_chan
    rc = -(-k * k // (16 * n_plane)) * 8
    args = dict(
        charges=charges, basis=basis, leaf=atom_leaf.reshape(1, atoms), leaf_lists=leaf_lists,
        coarse_lists=coarse_lists, up=up_ops, down=down_ops, leaf_ops=leaf_ops, coarse_ops=coarse_ops,
        mix=mix, cot=cotangent,
    )
    outs = dict(
        pot_all=shape((n_chan * CH, atoms), BF16),
        total_out=shape((2 * n_plane * rc, 128), F32),
    )
    copies = 2 * (n_chan - 1) + 4 + 2 + 2 * (n_plane - 1) + n_z - 1
    scratch = dict(
        cot_all=((n_chan * CH, atoms), BF16),
        basis_pad=((KP, atoms), F32),
        member=((LD, atoms), BF16),
        octants=((1024, 1024), BF16),
        stack=((8 * KP, CH * CD), BF16),
        back_pot=((CH, atoms), BF16),
        src=((CH * KP, 2 * LD), BF16),
        csrc=((4 * KP, 256), BF16),
        bexp=((CH * KP, LD), BF16),
        back=((KP, CH * LD), BF16),
        bfar=((KP, CH * CD), BF16),
        to_left=((512, LD), BF16),
        to_right=((512, LD), BF16),
        from_right=((512, LD), BF16),
        from_left=((512, LD), BF16),
        coarse=((KP, CH * CD), BF16),
        coarse_right=((KP, CH * CD), BF16),
        coarse_left=((KP, CH * CD), BF16),
        up_pad=((8 * KP, KP), F32),
        down_pad=((8 * KP, KP), F32),
        lists=((slots, LD), jnp.int32),
        clists=((slots, 128), jnp.int32),
        picked=((slots * KP, CH * LD), BF16),
        cpicked=((slots * KP, CH * CD), BF16),
        child=((8 * KP, CH * LD), BF16),
        near=((KP, CH * LD), F32),
        far=((KP, CH * CD), F32),
        total=((KP * KP, 128), F32),
        slots=((2 * slots * KP, 128), F32),
        ops=((2 * slots * KP, KP), BF16),
        grad=((2 * n_plane * rc, 128), F32),
        half_in=((n_plane * rc, 128), F32),
        half=((n_plane * rc, 128), F32),
        part_in=((n_plane - 1, rc, 128), F32),
        part=((rc, 128), F32),
        z_in=((n_z, rc, 128), F32),
        pot=((CH, atoms), BF16),
    )
    names = tuple(args) + tuple(outs) + tuple(scratch) + ("sends", "recvs")
    pot_all, total = call(
        functools.partial(main_kernel, n_cells, n_chan, n_x, n_z, rc, names),
        list(outs.values()),
        [pltpu.VMEM(*v) for v in scratch.values()] + [pltpu.SemaphoreType.DMA((copies,))] * 2,
        tuple(args.values()),
        collective=0,
    )
    return call(
        final_kernel,
        [shape((CH, atoms), BF16), shape((k, k, slots), F32), shape((k, k, slots), F32)],
        [pltpu.VMEM(mix.shape, BF16)],
        (pot_all, total, charges, mix),
    )


def solution(mesh):
    n_cells, n_chan = mesh.shape["cells"], mesh.shape["chan"]
    n_x = 4 if n_cells % 8 == 0 and n_cells > 8 else 2
    n_z = n_cells // (2 * n_x)
    placed = (
        P("chan", "cells"),
        P(None, "cells"),
        P("cells"),
        P(None, "cells"),
        P(None, "cells"),
        P(),
        P(),
        P(),
        P(),
        P(),
        P("chan", "cells"),
    )
    return jax.shard_map(
        functools.partial(local, n_cells, n_chan, n_x, n_z),
        mesh=mesh,
        in_specs=placed,
        out_specs=(P("chan", "cells"), P(), P()),
        check_vma=False,
    )
```

```python
import functools

import jax
import jax.numpy as jnp
from jax import lax
from jax.experimental import pallas as pl
from jax.experimental.pallas import tpu as pltpu
from jax.sharding import PartitionSpec as P

MESH = pl.DeviceIdType.MESH
BF16 = jnp.bfloat16
F32 = jnp.float32
KP = 32
CH = 32
LD = 128
CD = 16
SG = 8
NN = (((1,), (0,)), ((), ()))
NT = (((1,), (1,)), ((), ()))
TN = (((0,), (0,)), ((), ()))


def dot(a, b, dims=NN):
    return lax.dot_general(a, b, dims, preferred_element_type=F32)


def one_hot(row, rows):
    index = lax.broadcasted_iota(jnp.int32, (rows, row.shape[1]), 0)
    return jnp.where(index == row, 1.0, 0.0).astype(BF16)


def lane_iota(rows, lanes):
    return lax.broadcasted_iota(jnp.int32, (rows, lanes), 1)


def fill_member(leaf_ref, member, first):
    member[...] = one_hot(leaf_ref[...] - first, LD)


def fill_basis(basis_ref, basis_pad):
    k = basis_ref.shape[0]
    basis_pad[...] = jnp.zeros_like(basis_pad)
    basis_pad[0:k, :] = basis_ref[...]


def fill_octants(octants):
    for o in range(8):
        lane = lane_iota(1, 128)
        row = (lane >> 4) * 128 + 8 * (lane & 15) + o
        octants[:, o * 128 : (o + 1) * 128] = one_hot(row, 1024)


def spread(values_ref, basis_pad, member, out):
    def block(b, carry):
        values = values_ref[pl.ds(pl.multiple_of(b * 16, 16), 16), :].astype(F32)
        for quad in range(4):
            scaled = jnp.concatenate(
                [
                    (basis_pad[...] * values[c : c + 1, :]).astype(BF16)
                    for c in range(quad * 4, quad * 4 + 4)
                ],
                axis=0,
            )
            row = pl.multiple_of(b * 512 + quad * 128, 128)
            out[pl.ds(row, 128), 0:LD] = dot(scaled, member[...], NT).astype(BF16)
        return carry

    lax.fori_loop(0, CH // 16, block, 0)


def to_parents(fields, octants, ops, dims, stack):
    wide = jnp.concatenate(
        [
            jnp.concatenate(
                [fields[(cb * 8 + c) * KP : (cb * 8 + c + 1) * KP, 0:LD] for c in range(8)], axis=1
            )
            for cb in range(4)
        ],
        axis=0,
    )
    for o in range(8):
        part = dot(wide, octants[:, o * 128 : (o + 1) * 128]).astype(BF16)
        for cb in range(4):
            stack[o * KP : (o + 1) * KP, cb * 128 : (cb + 1) * 128] = part[cb * KP : (cb + 1) * KP]
    return dot(ops, stack[...], dims).astype(BF16)


def gather_group(lists, group, source, picked, base):
    rows = lists[pl.ds(pl.multiple_of(group * SG, SG), SG), :]
    blocks = source.shape[0] // KP
    for pair in range(SG // 2):
        hot = jnp.concatenate(
            [one_hot(rows[s : s + 1, :], 256) for s in (2 * pair, 2 * pair + 1)], axis=1
        )
        for part in range(0, blocks, 4):
            got = dot(source[part * KP : (part + 4) * KP, :], hot).astype(BF16)
            for half in range(2):
                s = 2 * pair + half
                for i in range(4):
                    c = part + i
                    picked[pl.ds(base + s * KP, KP), c * 128 : (c + 1) * 128] = got[
                        i * KP : (i + 1) * KP, half * 128 : (half + 1) * 128
                    ]


def group_rows(g):
    return pl.ds(pl.multiple_of(g * SG * KP, SG * KP), SG * KP)


def turn_ops(leaf_ops_ref, coarse_ops_ref, rows, turned, ops):
    k, _, s = leaf_ops_ref.shape
    rows[...] = jnp.zeros_like(rows)
    turned[...] = jnp.zeros_like(turned)
    for i in range(k):
        both = jnp.concatenate([leaf_ops_ref[i].astype(F32), coarse_ops_ref[i].astype(F32)], axis=1)
        rows[i * KP : i * KP + k, :] = both
    for j in range(k):
        turned[pl.ds(j, 2 * s, stride=KP), 0:KP] = rows[pl.ds(j, KP, stride=KP), :].T
    ops[...] = turned[:, 0:KP].astype(BF16)


def main_kernel(n_cells, n_chan, n_x, n_z, rc_a, rc_b, names, *refs):
    r = dict(zip(names, refs))
    cells = lax.axis_index("cells")
    chan = lax.axis_index("chan")
    core = lax.rem(cells, 2)
    x = lax.rem(cells // 2, n_x)
    z = cells // (2 * n_x)
    n_plane = n_x * n_chan
    m = x * n_chan + chan
    k = r["basis"].shape[0]
    n_slots = r["leaf_lists"].shape[0]
    groups = n_slots // SG
    left = (lax.rem(cells + n_cells - 1, n_cells), chan)
    right = (lax.rem(cells + 1, n_cells), chan)
    other = (cells + 1 - 2 * core, chan)
    chan_peers = [(cells, lax.rem(chan + i, n_chan)) for i in range(1, n_chan)]
    plane_peers, z_peers = [], []
    for i in range(1, n_plane):
        d = lax.rem(m + i, n_plane)
        plane_peers.append((d, ((z * n_x + d // n_chan) * 2 + core, lax.rem(d, n_chan))))
    for i in range(1, n_z):
        d = lax.rem(z + i, n_z)
        z_peers.append((d, ((d * n_x + x) * 2 + core, chan)))

    barrier = pltpu.get_barrier_semaphore()
    greeted = chan_peers + [left, right, other] + [d for _, d in plane_peers] + [d for _, d in z_peers]
    for device in greeted:
        pl.semaphore_signal(barrier, inc=1, device_id=device, device_id_type=MESH)

    sems = {"next": 0}

    def send(source, target, device):
        i = sems["next"]
        sems["next"] = i + 1
        copy = pltpu.make_async_remote_copy(
            src_ref=source,
            dst_ref=target,
            send_sem=r["sends"].at[i],
            recv_sem=r["recvs"].at[i],
            device_id=device,
            device_id_type=MESH,
        )
        copy.start()
        return copy

    member, basis_pad, src, bexp = r["member"], r["basis_pad"], r["src"], r["bexp"]
    fill_member(r["leaf"], member, cells * LD)
    fill_basis(r["basis"], basis_pad)
    pl.semaphore_wait(barrier, len(greeted))

    mine = pl.ds(pl.multiple_of(chan * CH, CH), CH)
    cot_copies = [send(r["cot"], r["cot_all"].at[mine, :], d) for d in chan_peers]

    spread(r["charges"], basis_pad, member, src)
    low = lane_iota(512, 128) < 64
    top = src[0:512, 0:LD].astype(F32)
    bottom = pltpu.roll(src[512:1024, 0:LD].astype(F32), 64, 1)
    r["to_left"][...] = jnp.where(low, top, bottom).astype(BF16)
    r["to_right"][...] = jnp.where(low, bottom, top).astype(BF16)
    halo = [send(r["to_left"], r["from_right"], left), send(r["to_right"], r["from_left"], right)]

    for ops_ref, pad, rows in ((r["up"], r["up_pad"], r["up_rows"]), (r["down"], r["down_pad"], r["down_rows"])):
        pad[...] = jnp.zeros_like(pad)
        for i in range(k):
            rows[i * 8 : (i + 1) * 8, 0:k] = ops_ref[i].astype(F32)
        for o in range(8):
            pad[o * KP : o * KP + k, 0:k] = rows[pl.ds(o, k, stride=8), :][:, 0:k]
    fill_octants(r["octants"])

    up_wide = jnp.concatenate([r["up_pad"][o * KP : (o + 1) * KP, :] for o in range(8)], axis=1).astype(BF16)
    down_wide = jnp.concatenate([r["down_pad"][o * KP : (o + 1) * KP, :] for o in range(8)], axis=1).astype(BF16)
    down_tall = r["down_pad"][...].astype(BF16)

    coarse = r["coarse"]
    coarse[...] = to_parents(src, r["octants"], up_wide, NN, r["stack"])
    coarse_halo = [send(coarse, r["coarse_right"], left), send(coarse, r["coarse_left"], right)]

    raw = r["leaf_lists"][...]
    r["lists"][...] = jnp.where(raw < 0, -1, (raw - cells * LD) & 255)
    raw = r["coarse_lists"][...]
    raw = jnp.concatenate([raw] * 8, axis=0).T
    at = jnp.where(raw < 0, -1, (raw - cells * CD) & 31)
    c8 = (lane_iota(n_slots, 128) >> 4) * CD
    r["clists"][...] = jnp.where(at < 0, -1, jnp.where(at < CD, c8 + at, 112 + c8 + at))

    r["cot_all"][mine, :] = r["cot"][...]
    for copy in cot_copies:
        copy.wait()
    r["back_pot"][...] = dot(r["mix"][mine, :], r["cot_all"][...]).astype(BF16)
    spread(r["back_pot"], basis_pad, member, bexp)
    r["bfar"][...] = to_parents(bexp, r["octants"], down_tall, TN, r["stack"])
    for c in range(CH):
        r["back"][:, c * LD : (c + 1) * LD] = bexp[c * KP : (c + 1) * KP, :]

    for copy in coarse_halo:
        copy.wait()
    first = (lane_iota(KP, 128) & 15) < 8
    csrc = r["csrc"]
    for cb in range(4):
        lanes = slice(cb * 128, (cb + 1) * 128)
        rows = slice(cb * KP, (cb + 1) * KP)
        csrc[rows, 0:128] = coarse[:, lanes]
        csrc[rows, 128:256] = jnp.where(
            first, r["coarse_right"][:, lanes].astype(F32), r["coarse_left"][:, lanes].astype(F32)
        ).astype(BF16)

    picked, cpicked, slots = (r["picked_even"], r["picked_odd"]), r["cpicked"], r["slots"]

    def coarse_group(h, carry):
        for i in range(2):
            g = 2 * h + i
            gather_group(r["clists"], g, csrc, cpicked, pl.multiple_of(g * SG * KP, SG * KP))
        return carry

    lax.fori_loop(0, groups // 2, coarse_group, 0)
    slots[groups * SG * KP : 2 * groups * SG * KP, 0:KP] = dot(cpicked[...], r["bfar"][...], NT)

    for copy in halo:
        copy.wait()
    a, b = r["from_right"][...].astype(F32), r["from_left"][...].astype(F32)
    src[0:512, LD : 2 * LD] = jnp.where(low, a, b).astype(BF16)
    src[512:1024, LD : 2 * LD] = pltpu.roll(jnp.where(low, b, a), 64, 1).astype(BF16)

    def leaf_group(h, carry):
        for i in range(2):
            gather_group(r["lists"], 2 * h + i, src, picked[i], pl.multiple_of(h * SG * KP, SG * KP))
            slots[group_rows(2 * h + i), 0:KP] = dot(picked[i][group_rows(h), :], r["back"][...], NT)
        return carry

    def pack(grad, first_row, unit):
        for jb in range(7):
            turned = jnp.concatenate(
                [slots[pl.ds(first_row + jb * 4 + i, 32, stride=KP), :] for i in range(4)], axis=0
            ).T
            grad[pl.ds(unit * 7 * k + jb, k, stride=7), :] = turned[0:k, :]

    class Exchange:
        def __init__(self, tag, rc, units):
            self.refs = {n: r[n + tag] for n in ("grad", "half_in", "half", "part_in", "part", "z_in", "total")}
            self.rc = rc
            self.size = n_plane * rc
            grad = self.refs["grad"]
            used = 7 * k * len(units) // 8 * 8
            grad[used:, :] = jnp.zeros((2 * self.size - used, 128), F32)
            for unit, row in enumerate(units):
                pack(grad, row, unit)
            self.core = send(
                grad.at[pl.ds(pl.multiple_of((1 - core) * self.size, 8), self.size), :],
                self.refs["half_in"],
                other,
            )

        def chunk(self, d):
            return pl.ds(pl.multiple_of(d * self.rc, 8), self.rc)

        def plane(self):
            self.core.wait()
            q = self.refs
            q["half"][...] = (
                q["grad"][pl.ds(pl.multiple_of(core * self.size, 8), self.size), :] + q["half_in"][...]
            )
            self.copies = [
                send(q["half"].at[self.chunk(d), :], q["part_in"].at[i], device)
                for i, (d, device) in enumerate(plane_peers)
            ]

        def depth(self):
            q = self.refs
            for copy in self.copies:
                copy.wait()
            summed = q["half"][self.chunk(m), :]
            for i in range(n_plane - 1):
                summed = summed + q["part_in"][i]
            q["part"][...] = summed
            self.copies = [send(q["part"], q["z_in"].at[z], device) for _, device in z_peers]
            q["z_in"][z] = summed

        def gather(self):
            q = self.refs
            for copy in self.copies:
                copy.wait()
            summed = q["z_in"][0]
            for i in range(1, n_z):
                summed = summed + q["z_in"][i]
            own = pl.ds(pl.multiple_of(core * self.size + m * self.rc, 8), self.rc)
            q["total"][own, :] = summed
            self.copies = [
                send(q["total"].at[own, :], q["total"].at[own, :], device) for _, device in plane_peers
            ]

        def last(self):
            for copy in self.copies:
                copy.wait()
            side = self.refs["total"].at[pl.ds(pl.multiple_of(core * self.size, 8), self.size), :]
            self.copies = [send(side, side, other)]

        def finish(self):
            for copy in self.copies:
                copy.wait()

    halfway = groups * SG * KP // 2
    lax.fori_loop(0, groups // 4, leaf_group, 0)
    early = Exchange("_a", rc_a, [2 * halfway, 3 * halfway, 0])
    lax.fori_loop(groups // 4, 3 * groups // 8, leaf_group, 0)
    early.plane()
    lax.fori_loop(3 * groups // 8, groups // 2, leaf_group, 0)
    late = Exchange("_b", rc_b, [halfway])

    turn_ops(r["leaf_ops"], r["coarse_ops"], r["ops_rows"], r["ops_turned"], r["ops"])
    late.plane()
    near = r["near"]
    far16 = dot(r["ops"][groups * SG * KP : 2 * groups * SG * KP, :], cpicked[...], TN).astype(BF16)

    far_rows = jnp.concatenate([far16[:, cb * 128 : (cb + 1) * 128] for cb in range(4)], axis=0)
    octant = lane_iota(KP, 128) & 7
    child = r["child"]
    for c in range(8):
        parent = (lane_iota(1, 128) >> 3) + c * CD
        wide = dot(far_rows, one_hot(parent, 128))
        for cb in range(4):
            lanes = slice((cb * 8 + c) * 128, (cb * 8 + c + 1) * 128)
            block = wide[cb * KP : (cb + 1) * KP, :]
            for o in range(8):
                child[o * KP : (o + 1) * KP, lanes] = jnp.where(octant == o, block, 0.0).astype(BF16)
    for c in range(0, CH * LD, 512):
        near[:, c : c + 512] = dot(down_wide, child[:, c : c + 512])

    def near_group(h, carry):
        even, odd = r["ops"][group_rows(2 * h), :], r["ops"][group_rows(2 * h + 1), :]
        for c in range(0, CH * LD, 512):
            lanes = slice(c, c + 512)
            near[:, lanes] += dot(even, picked[0][group_rows(h), lanes], TN) + dot(
                odd, picked[1][group_rows(h), lanes], TN
            )
        return carry

    lax.fori_loop(0, 1, near_group, 0)
    early.depth()
    lax.fori_loop(1, 3, near_group, 0)
    late.depth()
    lax.fori_loop(3, groups // 2, near_group, 0)

    expand = bexp
    for c in range(CH):
        expand[c * KP : (c + 1) * KP, :] = near[:, c * LD : (c + 1) * LD].astype(BF16)

    def collect(b, carry):
        rows = []
        for quad in range(4):
            row = pl.multiple_of(b * 512 + quad * 128, 128)
            per_atom = dot(expand[pl.ds(row, 128), :], member[...])
            for c in range(4):
                rows.append(
                    jnp.sum(
                        per_atom[c * KP : (c + 1) * KP, :] * basis_pad[...], axis=0, keepdims=True
                    )
                )
        pot[pl.ds(pl.multiple_of(b * 16, 16), 16), :] = jnp.concatenate(rows, axis=0).astype(BF16)
        return carry

    pot = r["pot"]
    lax.fori_loop(0, CH // 16, collect, 0)
    pot_all = r["pot_all"]
    pot_copies = [send(pot, pot_all.at[mine, :], d) for d in chan_peers]
    pot_all[mine, :] = pot[...]

    r["mixt"][...] = r["mix"][...].astype(F32).T.astype(BF16)
    early.gather()
    late.gather()
    for copy in pot_copies:
        copy.wait()
    r["refined"][...] = (
        r["charges"][...].astype(F32) + dot(r["mixt"][mine, :], pot_all[...])
    ).astype(BF16)
    early.last()
    late.last()
    early.finish()
    late.finish()


def final_kernel(refined_ref, early_ref, late_ref, out_ref, gl_ref, gc_ref):
    k = gl_ref.shape[0]
    out_ref[...] = refined_ref[...]
    unit = 7 * k

    def rows(ref, u, i):
        return ref[u * unit + i * 7 : u * unit + (i + 1) * 7, :]

    for i in range(k):
        for out, low, high in (
            (gc_ref, rows(early_ref, 0, i), rows(early_ref, 1, i)),
            (gl_ref, rows(early_ref, 2, i), rows(late_ref, 0, i)),
        ):
            for j in range(4):
                count = 7 if j == 0 else 6
                both = jnp.concatenate(
                    [low[0:count, j * 32 : (j + 1) * 32], high[0:count, j * 32 : (j + 1) * 32]], axis=1
                )
                out[i, pl.ds(j, count, stride=4), :] = both


VMEM = pl.BlockSpec(memory_space=pltpu.VMEM)


def call(kernel, outs, scratch, args, mib, collective=None):
    extra = {}
    if collective is not None:
        extra = dict(collective_id=collective, has_side_effects=True)
    return pl.pallas_call(
        kernel,
        out_shape=outs,
        in_specs=[VMEM] * len(args),
        out_specs=[VMEM] * len(outs),
        scratch_shapes=scratch,
        compiler_params=pltpu.CompilerParams(vmem_limit_bytes=mib << 20, **extra),
    )(*args)


def local(n_cells, n_chan, n_x, n_z, charges, basis, atom_leaf, leaf_lists, coarse_lists, up_ops, down_ops, leaf_ops,
          coarse_ops, mix, cotangent):
    k, atoms = basis.shape
    slots = leaf_lists.shape[0]
    shape = jax.ShapeDtypeStruct
    n_plane = n_x * n_chan
    rc_a, rc_b = (-(-units * 7 * k // (16 * n_plane)) * 8 for units in (3, 1))
    args = dict(
        charges=charges, basis=basis, leaf=atom_leaf.reshape(1, atoms), leaf_lists=leaf_lists,
        coarse_lists=coarse_lists.T, up=jnp.transpose(up_ops, (1, 0, 2)), down=jnp.transpose(down_ops, (1, 0, 2)), leaf_ops=leaf_ops, coarse_ops=coarse_ops,
        mix=mix, cot=cotangent,
    )
    outs = dict(
        refined=shape((CH, atoms), BF16),
        total_a=shape((2 * n_plane * rc_a, 128), F32),
        total_b=shape((2 * n_plane * rc_b, 128), F32),
    )
    copies = 2 * (n_chan - 1) + 4 + 2 * (2 + 2 * (n_plane - 1) + n_z - 1)
    scratch = dict(
        cot_all=((n_chan * CH, atoms), BF16),
        basis_pad=((KP, atoms), F32),
        member=((LD, atoms), BF16),
        octants=((1024, 1024), BF16),
        stack=((8 * KP, CH * CD), BF16),
        back_pot=((CH, atoms), BF16),
        src=((CH * KP, 2 * LD), BF16),
        csrc=((4 * KP, 256), BF16),
        bexp=((CH * KP, LD), BF16),
        back=((KP, CH * LD), BF16),
        bfar=((KP, CH * CD), BF16),
        to_left=((512, LD), BF16),
        to_right=((512, LD), BF16),
        from_right=((512, LD), BF16),
        from_left=((512, LD), BF16),
        coarse=((KP, CH * CD), BF16),
        coarse_right=((KP, CH * CD), BF16),
        coarse_left=((KP, CH * CD), BF16),
        up_pad=((8 * KP, KP), F32),
        down_pad=((8 * KP, KP), F32),
        lists=((slots, LD), jnp.int32),
        clists=((slots, 128), jnp.int32),
        picked_even=((slots * KP // 2, CH * LD), BF16),
        picked_odd=((slots * KP // 2, CH * LD), BF16),
        cpicked=((slots * KP, CH * CD), BF16),
        child=((8 * KP, CH * LD), BF16),
        near=((KP, CH * LD), F32),
        up_rows=((8 * k, 128), F32),
        down_rows=((8 * k, 128), F32),
        pot_all=((n_chan * CH, atoms), BF16),
        mixt=(mix.shape, BF16),
        ops_rows=((KP * KP, 128), F32),
        ops_turned=((2 * slots * KP, 128), F32),
        slots=((2 * slots * KP, 128), F32),
        ops=((2 * slots * KP, KP), BF16),
        pot=((CH, atoms), BF16),
    )
    for tag, rc in (("_a", rc_a), ("_b", rc_b)):
        scratch["grad" + tag] = ((2 * n_plane * rc, 128), F32)
        scratch["half_in" + tag] = ((n_plane * rc, 128), F32)
        scratch["half" + tag] = ((n_plane * rc, 128), F32)
        scratch["part_in" + tag] = ((n_plane - 1, rc, 128), F32)
        scratch["part" + tag] = ((rc, 128), F32)
        scratch["z_in" + tag] = ((n_z, rc, 128), F32)
    names = tuple(args) + tuple(outs) + tuple(scratch) + ("sends", "recvs")
    refined, early, late = call(
        functools.partial(main_kernel, n_cells, n_chan, n_x, n_z, rc_a, rc_b, names),
        list(outs.values()),
        [pltpu.VMEM(*v) for v in scratch.values()] + [pltpu.SemaphoreType.DMA((copies,))] * 2,
        tuple(args.values()),
        40,
        collective=0,
    )
    return call(
        final_kernel,
        [shape((CH, atoms), BF16), shape((k, k, slots), F32), shape((k, k, slots), F32)],
        [],
        (refined, early, late),
        8,
    )


def solution(mesh):
    n_cells, n_chan = mesh.shape["cells"], mesh.shape["chan"]
    n_x = 4 if n_cells % 8 == 0 and n_cells > 8 else 2
    n_z = n_cells // (2 * n_x)
    placed = (
        P("chan", "cells"),
        P(None, "cells"),
        P("cells"),
        P(None, "cells"),
        P(None, "cells"),
        P(),
        P(),
        P(),
        P(),
        P(),
        P("chan", "cells"),
    )
    return jax.shard_map(
        functools.partial(local, n_cells, n_chan, n_x, n_z),
        mesh=mesh,
        in_specs=placed,
        out_specs=(P("chan", "cells"), P(), P()),
        check_vma=False,
    )
```

```python
import functools

import jax
import jax.numpy as jnp
from jax import lax
from jax.experimental import pallas as pl
from jax.experimental.pallas import tpu as pltpu
from jax.sharding import PartitionSpec as P

MESH = pl.DeviceIdType.MESH
BF16 = jnp.bfloat16
F32 = jnp.float32
ARGS = ("leaf", "basis", "charges", "cot", "up", "down", "leaf_lists", "coarse_lists", "leaf_ops", "coarse_ops", "mix")
KP = 32
CH = 32
LD = 128
CD = 16
SG = 8
NN = (((1,), (0,)), ((), ()))
NT = (((1,), (1,)), ((), ()))
TN = (((0,), (0,)), ((), ()))


def dot(a, b, dims=NN):
    return lax.dot_general(a, b, dims, preferred_element_type=F32)


def one_hot(row, rows):
    index = lax.broadcasted_iota(jnp.int32, (rows, row.shape[1]), 0)
    return jnp.where(index == row, 1.0, 0.0).astype(BF16)


def lane_iota(rows, lanes):
    return lax.broadcasted_iota(jnp.int32, (rows, lanes), 1)


def fill_member(leaf_ref, member, first):
    member[...] = one_hot(leaf_ref[...] - first, LD)


def fill_basis(basis_ref, basis_pad):
    k = basis_ref.shape[0]
    basis_pad[...] = jnp.zeros_like(basis_pad)
    basis_pad[0:k, :] = basis_ref[...]


def fill_octants(octants):
    for o in range(8):
        lane = lane_iota(1, 128)
        row = (lane >> 4) * 128 + 8 * (lane & 15) + o
        octants[:, o * 128 : (o + 1) * 128] = one_hot(row, 1024)


def spread(values_ref, basis_pad, member, out):
    def block(b, carry):
        values = values_ref[pl.ds(pl.multiple_of(b * 16, 16), 16), :].astype(F32)
        for quad in range(4):
            scaled = jnp.concatenate(
                [
                    (basis_pad[...] * values[c : c + 1, :]).astype(BF16)
                    for c in range(quad * 4, quad * 4 + 4)
                ],
                axis=0,
            )
            row = pl.multiple_of(b * 512 + quad * 128, 128)
            out[pl.ds(row, 128), 0:LD] = dot(scaled, member[...], NT).astype(BF16)
        return carry

    lax.fori_loop(0, CH // 16, block, 0)


def to_parents(fields, octants, ops, dims, stack):
    wide = jnp.concatenate(
        [
            jnp.concatenate(
                [fields[(cb * 8 + c) * KP : (cb * 8 + c + 1) * KP, 0:LD] for c in range(8)], axis=1
            )
            for cb in range(4)
        ],
        axis=0,
    )
    for o in range(8):
        part = dot(wide, octants[:, o * 128 : (o + 1) * 128]).astype(BF16)
        for cb in range(4):
            stack[o * KP : (o + 1) * KP, cb * 128 : (cb + 1) * 128] = part[cb * KP : (cb + 1) * KP]
    return dot(ops, stack[...], dims).astype(BF16)


def gather_group(lists, group, source, picked, base):
    rows = lists[pl.ds(pl.multiple_of(group * SG, SG), SG), :]
    blocks = source.shape[0] // KP
    for pair in range(SG // 2):
        hot = jnp.concatenate(
            [one_hot(rows[s : s + 1, :], 256) for s in (2 * pair, 2 * pair + 1)], axis=1
        )
        for part in range(0, blocks, 4):
            got = dot(source[part * KP : (part + 4) * KP, :], hot).astype(BF16)
            for half in range(2):
                s = 2 * pair + half
                for i in range(4):
                    c = part + i
                    picked[pl.ds(base + s * KP, KP), c * 128 : (c + 1) * 128] = got[
                        i * KP : (i + 1) * KP, half * 128 : (half + 1) * 128
                    ]


def group_rows(g):
    return pl.ds(pl.multiple_of(g * SG * KP, SG * KP), SG * KP)


def turn_ops(leaf_ops_ref, coarse_ops_ref, rows, turned, ops):
    k, _, s = leaf_ops_ref.shape
    rows[...] = jnp.zeros_like(rows)
    turned[...] = jnp.zeros_like(turned)
    for i in range(k):
        both = jnp.concatenate([leaf_ops_ref[i].astype(F32), coarse_ops_ref[i].astype(F32)], axis=1)
        rows[i * KP : i * KP + k, :] = both
    for j in range(k):
        turned[pl.ds(j, 2 * s, stride=KP), 0:KP] = rows[pl.ds(j, KP, stride=KP), :].T
    ops[...] = turned[:, 0:KP].astype(BF16)


def main_kernel(n_cells, n_chan, n_x, n_z, rc, names, *refs):
    r = dict(zip(names, refs))
    cells = lax.axis_index("cells")
    chan = lax.axis_index("chan")
    core = lax.rem(cells, 2)
    x = lax.rem(cells // 2, n_x)
    z = cells // (2 * n_x)
    n_plane = 2 * n_x * n_chan
    m = (x * n_chan + chan) * 2 + core
    k = r["basis_hbm"].shape[0]
    n_slots = r["leaf_lists_hbm"].shape[0]
    groups = n_slots // SG
    left = (lax.rem(cells + n_cells - 1, n_cells), chan)
    right = (lax.rem(cells + 1, n_cells), chan)
    chan_peers = [(cells, lax.rem(chan + i, n_chan)) for i in range(1, n_chan)]
    plane_peers, z_peers = [], []
    for i in range(1, n_plane):
        d = lax.rem(m + i, n_plane)
        place = d // 2
        plane_peers.append(
            (d, ((z * n_x + place // n_chan) * 2 + lax.rem(d, 2), lax.rem(place, n_chan)))
        )
    for i in range(1, n_z):
        d = lax.rem(z + i, n_z)
        z_peers.append((d, ((d * n_x + x) * 2 + core, chan)))

    barrier = pltpu.get_barrier_semaphore()
    greeted = chan_peers + [left, right] + [d for _, d in plane_peers] + [d for _, d in z_peers]
    for device in greeted:
        pl.semaphore_signal(barrier, inc=1, device_id=device, device_id_type=MESH)

    pending = {}
    for i, name in enumerate(ARGS):
        if name == "cot":
            target = r["cot_all"].at[pl.ds(pl.multiple_of(chan * CH, CH), CH), :]
        else:
            target = r[name]
        pending[name] = pltpu.make_async_copy(r[name + "_hbm"], target, r["loads"].at[i])
        pending[name].start()

    def load(*names):
        for name in names:
            pending.pop(name).wait()

    sems = {"next": 0}

    def send(source, target, device):
        i = sems["next"]
        sems["next"] = i + 1
        copy = pltpu.make_async_remote_copy(
            src_ref=source,
            dst_ref=target,
            send_sem=r["sends"].at[i],
            recv_sem=r["recvs"].at[i],
            device_id=device,
            device_id_type=MESH,
        )
        copy.start()
        return copy

    member, basis_pad, src, bexp = r["member"], r["basis_pad"], r["src"], r["bexp"]
    load("leaf", "basis")
    fill_member(r["leaf"], member, cells * LD)
    fill_basis(r["basis"], basis_pad)
    pl.semaphore_wait(barrier, len(greeted))

    mine = pl.ds(pl.multiple_of(chan * CH, CH), CH)
    cot_copies = [send(r["cot_hbm"], r["cot_all"].at[mine, :], d) for d in chan_peers]

    load("charges")
    spread(r["charges"], basis_pad, member, src)
    low = lane_iota(512, 128) < 64
    top = src[0:512, 0:LD].astype(F32)
    bottom = pltpu.roll(src[512:1024, 0:LD].astype(F32), 64, 1)
    r["to_left"][...] = jnp.where(low, top, bottom).astype(BF16)
    r["to_right"][...] = jnp.where(low, bottom, top).astype(BF16)
    halo = [send(r["to_left"], r["from_right"], left), send(r["to_right"], r["from_left"], right)]

    load("up", "down")
    for ops_ref, pad, rows in ((r["up"], r["up_pad"], r["up_rows"]), (r["down"], r["down_pad"], r["down_rows"])):
        pad[...] = jnp.zeros_like(pad)
        for i in range(k):
            rows[i * 8 : (i + 1) * 8, 0:k] = ops_ref[i].astype(F32)
        for o in range(8):
            pad[o * KP : o * KP + k, 0:k] = rows[pl.ds(o, k, stride=8), :][:, 0:k]
    fill_octants(r["octants"])

    up_wide = jnp.concatenate([r["up_pad"][o * KP : (o + 1) * KP, :] for o in range(8)], axis=1).astype(BF16)
    down_wide = jnp.concatenate([r["down_pad"][o * KP : (o + 1) * KP, :] for o in range(8)], axis=1).astype(BF16)
    down_tall = r["down_pad"][...].astype(BF16)

    coarse = r["coarse"]
    coarse[...] = to_parents(src, r["octants"], up_wide, NN, r["stack"])
    coarse_halo = [send(coarse, r["coarse_right"], left), send(coarse, r["coarse_left"], right)]

    load("leaf_lists", "coarse_lists", "leaf_ops", "coarse_ops", "mix", "cot")
    raw = r["leaf_lists"][...]
    r["lists"][...] = jnp.where(raw < 0, -1, (raw - cells * LD) & 255)
    raw = r["coarse_lists"][...]
    raw = jnp.concatenate([raw] * 8, axis=0).T
    at = jnp.where(raw < 0, -1, (raw - cells * CD) & 31)
    c8 = (lane_iota(n_slots, 128) >> 4) * CD
    r["clists"][...] = jnp.where(at < 0, -1, jnp.where(at < CD, c8 + at, 112 + c8 + at))

    turn_ops(r["leaf_ops"], r["coarse_ops"], r["ops_rows"], r["ops_turned"], r["ops"])
    r["mixt"][...] = r["mix"][...].astype(F32).T.astype(BF16)

    for copy in halo:
        copy.wait()
    a, b = r["from_right"][...].astype(F32), r["from_left"][...].astype(F32)
    src[0:512, LD : 2 * LD] = jnp.where(low, a, b).astype(BF16)
    src[512:1024, LD : 2 * LD] = pltpu.roll(jnp.where(low, b, a), 64, 1).astype(BF16)
    picked, cpicked, slots = r["picked"], r["cpicked"], r["slots"]

    def leaf_gather(g, carry):
        gather_group(r["lists"], g, src, picked, pl.multiple_of(g * SG * KP, SG * KP))
        return carry

    def leaf_gradient(g, carry):
        slots[group_rows(g), 0:KP] = dot(picked[group_rows(g), :], r["back"][...], NT)
        return carry

    lax.fori_loop(0, 2, leaf_gather, 0)

    for copy in cot_copies:
        copy.wait()
    r["back_pot"][...] = dot(r["mix"][mine, :], r["cot_all"][...]).astype(BF16)
    spread(r["back_pot"], basis_pad, member, bexp)
    for c in range(CH):
        r["back"][:, c * LD : (c + 1) * LD] = bexp[c * KP : (c + 1) * KP, :]
    r["bfar"][...] = to_parents(bexp, r["octants"], down_tall, TN, r["stack"])

    for copy in coarse_halo:
        copy.wait()
    first = (lane_iota(KP, 128) & 15) < 8
    csrc = r["csrc"]
    for cb in range(4):
        lanes = slice(cb * 128, (cb + 1) * 128)
        rows = slice(cb * KP, (cb + 1) * KP)
        csrc[rows, 0:128] = coarse[:, lanes]
        csrc[rows, 128:256] = jnp.where(
            first, r["coarse_right"][:, lanes].astype(F32), r["coarse_left"][:, lanes].astype(F32)
        ).astype(BF16)

    def coarse_group(h, carry):
        for i in range(2):
            g = 2 * h + i
            gather_group(r["clists"], g, csrc, cpicked, pl.multiple_of(g * SG * KP, SG * KP))
        return carry

    lax.fori_loop(0, groups // 2, coarse_group, 0)
    slots[groups * SG * KP : 2 * groups * SG * KP, 0:KP] = dot(cpicked[...], r["bfar"][...], NT)

    def leaf_group(g, carry):
        leaf_gather(g, 0)
        return leaf_gradient(g, 0)

    lax.fori_loop(0, 2, leaf_gradient, 0)
    lax.fori_loop(2, groups, leaf_group, 0)

    grad, part_in, z_in, total = r["grad"], r["part_in"], r["z_in"], r["total"]
    used = k * k // 8 * 8
    grad[used:, :] = jnp.zeros((n_plane * rc - used, 128), F32)
    for j in range(k):
        turned = slots[pl.ds(j, 2 * n_slots, stride=KP), :].T
        grad[pl.ds(j, k, stride=k), :] = turned[0:k, :]

    def chunk(d):
        return pl.ds(pl.multiple_of(d * rc, 8), rc)

    plane_copies = [
        send(grad.at[chunk(d), :], part_in.at[i], device) for i, (d, device) in enumerate(plane_peers)
    ]

    near = r["near"]
    far16 = dot(r["ops"][groups * SG * KP : 2 * groups * SG * KP, :], cpicked[...], TN).astype(BF16)

    far_rows = jnp.concatenate([far16[:, cb * 128 : (cb + 1) * 128] for cb in range(4)], axis=0)
    octant = lane_iota(KP, 128) & 7
    child = r["child"]
    for c in range(8):
        parent = (lane_iota(1, 128) >> 3) + c * CD
        wide = dot(far_rows, one_hot(parent, 128))
        for cb in range(4):
            lanes = slice((cb * 8 + c) * 128, (cb * 8 + c + 1) * 128)
            block = wide[cb * KP : (cb + 1) * KP, :]
            for o in range(8):
                child[o * KP : (o + 1) * KP, lanes] = jnp.where(octant == o, block, 0.0).astype(BF16)
    for c in range(0, CH * LD, 512):
        near[:, c : c + 512] = dot(down_wide, child[:, c : c + 512])

    def near_group(g, carry):
        ops = r["ops"][group_rows(g), :]
        for c in range(0, CH * LD, 512):
            near[:, c : c + 512] += dot(ops, picked[group_rows(g), c : c + 512], TN)
        return carry

    lax.fori_loop(0, 6, near_group, 0)
    for copy in plane_copies:
        copy.wait()
    summed = grad[chunk(m), :]
    for i in range(n_plane - 1):
        summed = summed + part_in[i]
    r["part"][...] = summed
    z_copies = [send(r["part"], z_in.at[z], device) for _, device in z_peers]
    z_in[z] = summed
    lax.fori_loop(6, groups, near_group, 0)

    expand = bexp
    for c in range(CH):
        expand[c * KP : (c + 1) * KP, :] = near[:, c * LD : (c + 1) * LD].astype(BF16)

    def collect(b, carry):
        rows = []
        for quad in range(4):
            row = pl.multiple_of(b * 512 + quad * 128, 128)
            per_atom = dot(expand[pl.ds(row, 128), :], member[...])
            for c in range(4):
                rows.append(
                    jnp.sum(
                        per_atom[c * KP : (c + 1) * KP, :] * basis_pad[...], axis=0, keepdims=True
                    )
                )
        pot[pl.ds(pl.multiple_of(b * 16, 16), 16), :] = jnp.concatenate(rows, axis=0).astype(BF16)
        return carry

    pot = r["pot"]
    lax.fori_loop(0, CH // 16, collect, 0)
    pot_all = r["pot_all"]
    pot_copies = [send(pot, pot_all.at[mine, :], d) for d in chan_peers]
    pot_all[mine, :] = pot[...]

    for copy in z_copies:
        copy.wait()
    summed = z_in[0]
    for i in range(1, n_z):
        summed = summed + z_in[i]
    total[chunk(m), :] = summed
    gather_copies = [send(total.at[chunk(m), :], total.at[chunk(m), :], device) for _, device in plane_peers]

    for copy in pot_copies:
        copy.wait()
    r["refined"][...] = (
        r["charges"][...].astype(F32) + dot(r["mixt"][mine, :], pot_all[...])
    ).astype(BF16)
    for copy in gather_copies:
        copy.wait()


def final_kernel(refined_ref, total_ref, out_ref, gl_ref, gc_ref):
    k, _, slots = gl_ref.shape
    out_ref[...] = refined_ref[...]
    for i in range(k):
        block = total_ref[i * k : (i + 1) * k, :]
        gl_ref[i] = block[:, 0:slots]
        gc_ref[i] = pltpu.roll(block, 128 - slots, 1)[:, 0:slots]


VMEM = pl.BlockSpec(memory_space=pltpu.VMEM)
HBM = pl.BlockSpec(memory_space=pltpu.HBM)


def call(kernel, outs, scratch, args, mib, space, collective=None):
    extra = {}
    if collective is not None:
        extra = dict(collective_id=collective, has_side_effects=True)
    return pl.pallas_call(
        kernel,
        out_shape=outs,
        in_specs=[space] * len(args),
        out_specs=[VMEM] * len(outs),
        scratch_shapes=scratch,
        compiler_params=pltpu.CompilerParams(vmem_limit_bytes=mib << 20, **extra),
    )(*args)


def local(n_cells, n_chan, n_x, n_z, charges, basis, atom_leaf, leaf_lists, coarse_lists, up_ops, down_ops, leaf_ops,
          coarse_ops, mix, cotangent):
    k, atoms = basis.shape
    slots = leaf_lists.shape[0]
    shape = jax.ShapeDtypeStruct
    n_plane = 2 * n_x * n_chan
    rc = -(-k * k // (8 * n_plane)) * 8
    args = dict(
        charges=charges, basis=basis, leaf=atom_leaf.reshape(1, atoms), leaf_lists=leaf_lists,
        coarse_lists=coarse_lists.T, up=jnp.transpose(up_ops, (1, 0, 2)), down=jnp.transpose(down_ops, (1, 0, 2)), leaf_ops=leaf_ops, coarse_ops=coarse_ops,
        mix=mix, cot=cotangent,
    )
    outs = dict(
        refined=shape((CH, atoms), BF16),
        total=shape((n_plane * rc, 128), F32),
    )
    copies = 2 * (n_chan - 1) + 4 + 2 * (n_plane - 1) + n_z - 1
    scratch = dict(
        cot_all=((n_chan * CH, atoms), BF16),
        basis_pad=((KP, atoms), F32),
        member=((LD, atoms), BF16),
        octants=((1024, 1024), BF16),
        stack=((8 * KP, CH * CD), BF16),
        back_pot=((CH, atoms), BF16),
        src=((CH * KP, 2 * LD), BF16),
        csrc=((4 * KP, 256), BF16),
        bexp=((CH * KP, LD), BF16),
        back=((KP, CH * LD), BF16),
        bfar=((KP, CH * CD), BF16),
        to_left=((512, LD), BF16),
        to_right=((512, LD), BF16),
        from_right=((512, LD), BF16),
        from_left=((512, LD), BF16),
        coarse=((KP, CH * CD), BF16),
        coarse_right=((KP, CH * CD), BF16),
        coarse_left=((KP, CH * CD), BF16),
        up_pad=((8 * KP, KP), F32),
        down_pad=((8 * KP, KP), F32),
        lists=((slots, LD), jnp.int32),
        clists=((slots, 128), jnp.int32),
        picked=((slots * KP, CH * LD), BF16),
        cpicked=((slots * KP, CH * CD), BF16),
        child=((8 * KP, CH * LD), BF16),
        near=((KP, CH * LD), F32),
        up_rows=((8 * k, 128), F32),
        down_rows=((8 * k, 128), F32),
        pot_all=((n_chan * CH, atoms), BF16),
        mixt=(mix.shape, BF16),
        ops_rows=((KP * KP, 128), F32),
        ops_turned=((2 * slots * KP, 128), F32),
        slots=((2 * slots * KP, 128), F32),
        ops=((2 * slots * KP, KP), BF16),
        pot=((CH, atoms), BF16),
        grad=((n_plane * rc, 128), F32),
        part_in=((n_plane - 1, rc, 128), F32),
        part=((rc, 128), F32),
        z_in=((n_z, rc, 128), F32),
    )
    for name, value in args.items():
        if name != "cot":
            scratch[name] = (value.shape, value.dtype)
    names = tuple(n + "_hbm" for n in ARGS) + tuple(outs) + tuple(scratch) + ("loads", "sends", "recvs")
    refined, total = call(
        functools.partial(main_kernel, n_cells, n_chan, n_x, n_z, rc, names),
        list(outs.values()),
        [pltpu.VMEM(*v) for v in scratch.values()]
        + [pltpu.SemaphoreType.DMA((n,)) for n in (len(args), copies, copies)],
        tuple(args[n] for n in ARGS),
        60,
        HBM,
        collective=0,
    )
    return call(
        final_kernel,
        [shape((CH, atoms), BF16), shape((k, k, slots), F32), shape((k, k, slots), F32)],
        [],
        (refined, total),
        60,
        VMEM,
    )


def solution(mesh):
    n_cells, n_chan = mesh.shape["cells"], mesh.shape["chan"]
    n_x = 4 if n_cells % 8 == 0 and n_cells > 8 else 2
    n_z = n_cells // (2 * n_x)
    placed = (
        P("chan", "cells"),
        P(None, "cells"),
        P("cells"),
        P(None, "cells"),
        P(None, "cells"),
        P(),
        P(),
        P(),
        P(),
        P(),
        P("chan", "cells"),
    )
    return jax.shard_map(
        functools.partial(local, n_cells, n_chan, n_x, n_z),
        mesh=mesh,
        in_specs=placed,
        out_specs=(P("chan", "cells"), P(), P()),
        check_vma=False,
    )
```

```python
import functools

import jax
import jax.numpy as jnp
from jax import lax
from jax.experimental import pallas as pl
from jax.experimental.pallas import tpu as pltpu
from jax.sharding import PartitionSpec as P

MESH = pl.DeviceIdType.MESH
BF16 = jnp.bfloat16
F32 = jnp.float32
ARGS = ("leaf", "basis", "charges", "cot", "up", "down", "leaf_lists", "coarse_lists", "leaf_ops", "coarse_ops", "mix")
KP = 32
CH = 32
LD = 128
CD = 16
SG = 8
NN = (((1,), (0,)), ((), ()))
NT = (((1,), (1,)), ((), ()))
TN = (((0,), (0,)), ((), ()))


def dot(a, b, dims=NN):
    return lax.dot_general(a, b, dims, preferred_element_type=F32)


def one_hot(row, rows):
    index = lax.broadcasted_iota(jnp.int32, (rows, row.shape[1]), 0)
    return jnp.where(index == row, 1.0, 0.0).astype(BF16)


def lane_iota(rows, lanes):
    return lax.broadcasted_iota(jnp.int32, (rows, lanes), 1)


def fill_member(leaf_ref, member, first):
    member[...] = one_hot(leaf_ref[...] - first, LD)


def fill_basis(basis_ref, basis_pad):
    k = basis_ref.shape[0]
    basis_pad[...] = jnp.zeros_like(basis_pad)
    basis_pad[0:k, :] = basis_ref[...]


def fill_octants(octants):
    for o in range(8):
        lane = lane_iota(1, 128)
        row = (lane >> 4) * 128 + 8 * (lane & 15) + o
        octants[:, o * 128 : (o + 1) * 128] = one_hot(row, 1024)


def spread(values_ref, basis_pad, member, out):
    def block(b, carry):
        values = values_ref[pl.ds(pl.multiple_of(b * 16, 16), 16), :].astype(F32)
        for quad in range(4):
            scaled = jnp.concatenate(
                [
                    (basis_pad[...] * values[c : c + 1, :]).astype(BF16)
                    for c in range(quad * 4, quad * 4 + 4)
                ],
                axis=0,
            )
            row = pl.multiple_of(b * 512 + quad * 128, 128)
            out[pl.ds(row, 128), 0:LD] = dot(scaled, member[...], NT).astype(BF16)
        return carry

    lax.fori_loop(0, CH // 16, block, 0)


def to_parents(fields, octants, ops, dims, stack):
    wide = jnp.concatenate(
        [
            jnp.concatenate(
                [fields[(cb * 8 + c) * KP : (cb * 8 + c + 1) * KP, 0:LD] for c in range(8)], axis=1
            )
            for cb in range(4)
        ],
        axis=0,
    )
    for o in range(8):
        part = dot(wide, octants[:, o * 128 : (o + 1) * 128]).astype(BF16)
        for cb in range(4):
            stack[o * KP : (o + 1) * KP, cb * 128 : (cb + 1) * 128] = part[cb * KP : (cb + 1) * KP]
    return dot(ops, stack[...], dims).astype(BF16)


def gather_group(lists, group, source, picked, base):
    rows = lists[pl.ds(pl.multiple_of(group * SG, SG), SG), :]
    blocks = source.shape[0] // KP
    for pair in range(SG // 2):
        hot = jnp.concatenate(
            [one_hot(rows[s : s + 1, :], 256) for s in (2 * pair, 2 * pair + 1)], axis=1
        )
        for part in range(0, blocks, 4):
            got = dot(source[part * KP : (part + 4) * KP, :], hot).astype(BF16)
            for half in range(2):
                s = 2 * pair + half
                for i in range(4):
                    c = part + i
                    picked[pl.ds(base + s * KP, KP), c * 128 : (c + 1) * 128] = got[
                        i * KP : (i + 1) * KP, half * 128 : (half + 1) * 128
                    ]


def group_rows(g):
    return pl.ds(pl.multiple_of(g * SG * KP, SG * KP), SG * KP)


def turn_ops(leaf_ops_ref, coarse_ops_ref, rows, turned, ops):
    k, _, s = leaf_ops_ref.shape
    rows[...] = jnp.zeros_like(rows)
    turned[...] = jnp.zeros_like(turned)
    for i in range(k):
        both = jnp.concatenate([leaf_ops_ref[i].astype(F32), coarse_ops_ref[i].astype(F32)], axis=1)
        rows[i * KP : i * KP + k, :] = both
    for j in range(k):
        turned[pl.ds(j, 2 * s, stride=KP), 0:KP] = rows[pl.ds(j, KP, stride=KP), :].T
    ops[...] = turned[:, 0:KP].astype(BF16)


def main_kernel(n_cells, n_chan, n_x, n_z, rc, names, *refs):
    r = dict(zip(names, refs))
    cells = lax.axis_index("cells")
    chan = lax.axis_index("chan")
    core = lax.rem(cells, 2)
    x = lax.rem(cells // 2, n_x)
    z = cells // (2 * n_x)
    n_plane = 2 * n_x * n_chan
    m = (x * n_chan + chan) * 2 + core
    k = r["basis_hbm"].shape[0]
    n_slots = r["leaf_lists_hbm"].shape[0]
    groups = n_slots // SG
    left = (lax.rem(cells + n_cells - 1, n_cells), chan)
    right = (lax.rem(cells + 1, n_cells), chan)
    chan_peers = [(cells, lax.rem(chan + i, n_chan)) for i in range(1, n_chan)]
    plane_peers, z_peers = [], []
    far_first = sorted(
        range(1, n_plane),
        key=lambda i: -min(i // (2 * n_chan), n_x - i // (2 * n_chan)) - min(i // 2 % n_chan, n_chan - i // 2 % n_chan),
    )
    for i in far_first:
        d = lax.rem(m + i, n_plane)
        place = d // 2
        plane_peers.append(
            (d, ((z * n_x + place // n_chan) * 2 + lax.rem(d, 2), lax.rem(place, n_chan)))
        )
    for i in sorted(range(1, n_z), key=lambda i: -min(i, n_z - i)):
        d = lax.rem(z + i, n_z)
        z_peers.append((d, ((d * n_x + x) * 2 + core, chan)))

    barrier = pltpu.get_barrier_semaphore()
    greeted = chan_peers + [left, right] + [d for _, d in plane_peers] + [d for _, d in z_peers]
    for device in greeted:
        pl.semaphore_signal(barrier, inc=1, device_id=device, device_id_type=MESH)

    pending = {}
    for i, name in enumerate(ARGS):
        if name == "cot":
            target = r["cot_all"].at[pl.ds(pl.multiple_of(chan * CH, CH), CH), :]
        else:
            target = r[name]
        pending[name] = pltpu.make_async_copy(r[name + "_hbm"], target, r["loads"].at[i])
        pending[name].start()

    def load(*names):
        for name in names:
            pending.pop(name).wait()

    sems = {"next": 0}

    def send(source, target, device):
        i = sems["next"]
        sems["next"] = i + 1
        copy = pltpu.make_async_remote_copy(
            src_ref=source,
            dst_ref=target,
            send_sem=r["sends"].at[i],
            recv_sem=r["recvs"].at[i],
            device_id=device,
            device_id_type=MESH,
        )
        copy.start()
        return copy

    member, basis_pad, src, bexp = r["member"], r["basis_pad"], r["src"], r["bexp"]
    load("leaf", "basis")
    fill_member(r["leaf"], member, cells * LD)
    fill_basis(r["basis"], basis_pad)
    pl.semaphore_wait(barrier, len(greeted))

    mine = pl.ds(pl.multiple_of(chan * CH, CH), CH)
    cot_copies = [send(r["cot_hbm"], r["cot_all"].at[mine, :], d) for d in chan_peers]

    load("charges")
    spread(r["charges"], basis_pad, member, src)
    low = lane_iota(512, 128) < 64
    top = src[0:512, 0:LD].astype(F32)
    bottom = pltpu.roll(src[512:1024, 0:LD].astype(F32), 64, 1)
    r["to_left"][...] = jnp.where(low, top, bottom).astype(BF16)
    r["to_right"][...] = jnp.where(low, bottom, top).astype(BF16)
    halo = [send(r["to_left"], r["from_right"], left), send(r["to_right"], r["from_left"], right)]

    load("up", "down")
    for ops_ref, pad, rows in ((r["up"], r["up_pad"], r["up_rows"]), (r["down"], r["down_pad"], r["down_rows"])):
        pad[...] = jnp.zeros_like(pad)
        for i in range(k):
            rows[i * 8 : (i + 1) * 8, 0:k] = ops_ref[i].astype(F32)
        for o in range(8):
            pad[o * KP : o * KP + k, 0:k] = rows[pl.ds(o, k, stride=8), :][:, 0:k]
    fill_octants(r["octants"])

    up_wide = jnp.concatenate([r["up_pad"][o * KP : (o + 1) * KP, :] for o in range(8)], axis=1).astype(BF16)
    down_wide = jnp.concatenate([r["down_pad"][o * KP : (o + 1) * KP, :] for o in range(8)], axis=1).astype(BF16)
    down_tall = r["down_pad"][...].astype(BF16)

    coarse = r["coarse"]
    coarse[...] = to_parents(src, r["octants"], up_wide, NN, r["stack"])
    coarse_halo = [send(coarse, r["coarse_right"], left), send(coarse, r["coarse_left"], right)]

    load("leaf_lists", "coarse_lists", "leaf_ops", "coarse_ops", "mix", "cot")
    raw = r["leaf_lists"][...]
    r["lists"][...] = jnp.where(raw < 0, -1, (raw - cells * LD) & 255)
    raw = r["coarse_lists"][...]
    raw = jnp.concatenate([raw] * 8, axis=0).T
    at = jnp.where(raw < 0, -1, (raw - cells * CD) & 31)
    c8 = (lane_iota(n_slots, 128) >> 4) * CD
    r["clists"][...] = jnp.where(at < 0, -1, jnp.where(at < CD, c8 + at, 112 + c8 + at))


    for copy in halo:
        copy.wait()
    a, b = r["from_right"][...].astype(F32), r["from_left"][...].astype(F32)
    src[0:512, LD : 2 * LD] = jnp.where(low, a, b).astype(BF16)
    src[512:1024, LD : 2 * LD] = pltpu.roll(jnp.where(low, b, a), 64, 1).astype(BF16)
    picked, cpicked, slots = r["picked"], r["cpicked"], r["slots"]

    def leaf_gather(g, carry):
        gather_group(r["lists"], g, src, picked, pl.multiple_of(g * SG * KP, SG * KP))
        return carry

    def leaf_gradient(g, carry):
        slots[group_rows(g), 0:KP] = dot(picked[group_rows(g), :], r["back"][...], NT)
        return carry

    lax.fori_loop(0, 2, leaf_gather, 0)

    for copy in cot_copies:
        copy.wait()
    r["back_pot"][...] = dot(r["mix"][mine, :], r["cot_all"][...]).astype(BF16)
    spread(r["back_pot"], basis_pad, member, bexp)
    for c in range(CH):
        r["back"][:, c * LD : (c + 1) * LD] = bexp[c * KP : (c + 1) * KP, :]
    r["bfar"][...] = to_parents(bexp, r["octants"], down_tall, TN, r["stack"])

    for copy in coarse_halo:
        copy.wait()
    first = (lane_iota(KP, 128) & 15) < 8
    csrc = r["csrc"]
    for cb in range(4):
        lanes = slice(cb * 128, (cb + 1) * 128)
        rows = slice(cb * KP, (cb + 1) * KP)
        csrc[rows, 0:128] = coarse[:, lanes]
        csrc[rows, 128:256] = jnp.where(
            first, r["coarse_right"][:, lanes].astype(F32), r["coarse_left"][:, lanes].astype(F32)
        ).astype(BF16)

    def coarse_group(h, carry):
        for i in range(2):
            g = 2 * h + i
            gather_group(r["clists"], g, csrc, cpicked, pl.multiple_of(g * SG * KP, SG * KP))
        return carry

    lax.fori_loop(0, groups // 2, coarse_group, 0)
    slots[groups * SG * KP : 2 * groups * SG * KP, 0:KP] = dot(cpicked[...], r["bfar"][...], NT)

    def leaf_group(g, carry):
        leaf_gather(g, 0)
        return leaf_gradient(g, 0)

    lax.fori_loop(0, 2, leaf_gradient, 0)
    lax.fori_loop(2, groups, leaf_group, 0)

    grad, grad16, part_in, z_in, total = (r[n] for n in ("grad", "grad16", "part_in", "z_in", "total"))
    used = k * k // 8 * 8
    grad[used:, :] = jnp.zeros((n_plane * rc - used, 128), F32)
    for j in range(k):
        turned = slots[pl.ds(j, 2 * n_slots, stride=KP), :].T
        grad[pl.ds(j, k, stride=k), :] = turned[0:k, :]
    for d in range(n_plane):
        grad16[d] = grad[d * rc : (d + 1) * rc, :].astype(BF16)
    plane_copies = [
        send(grad16.at[d], part_in.at[i], device) for i, (d, device) in enumerate(plane_peers)
    ]

    turn_ops(r["leaf_ops"], r["coarse_ops"], r["ops_rows"], r["ops_turned"], r["ops"])
    r["mixt"][...] = r["mix"][...].astype(F32).T.astype(BF16)
    near = r["near"]
    far16 = dot(r["ops"][groups * SG * KP : 2 * groups * SG * KP, :], cpicked[...], TN).astype(BF16)

    far_rows = jnp.concatenate([far16[:, cb * 128 : (cb + 1) * 128] for cb in range(4)], axis=0)
    octant = lane_iota(KP, 128) & 7
    child = r["child"]
    for c in range(8):
        parent = (lane_iota(1, 128) >> 3) + c * CD
        wide = dot(far_rows, one_hot(parent, 128))
        for cb in range(4):
            lanes = slice((cb * 8 + c) * 128, (cb * 8 + c + 1) * 128)
            block = wide[cb * KP : (cb + 1) * KP, :]
            for o in range(8):
                child[o * KP : (o + 1) * KP, lanes] = jnp.where(octant == o, block, 0.0).astype(BF16)
    for c in range(0, CH * LD, 512):
        near[:, c : c + 512] = dot(down_wide, child[:, c : c + 512])

    def near_group(g, carry):
        ops = r["ops"][group_rows(g), :]
        for c in range(0, CH * LD, 512):
            near[:, c : c + 512] += dot(ops, picked[group_rows(g), c : c + 512], TN)
        return carry

    lax.fori_loop(0, groups // 2, near_group, 0)
    for copy in plane_copies:
        copy.wait()
    summed = grad[pl.ds(pl.multiple_of(m * rc, 8), rc), :]
    for i in range(n_plane - 1):
        summed = summed + part_in[i].astype(F32)
    r["part"][...] = summed.astype(BF16)
    z_copies = [send(r["part"], z_in.at[z], device) for _, device in z_peers]
    z_in[z] = summed.astype(BF16)
    lax.fori_loop(groups // 2, groups, near_group, 0)

    expand = bexp
    for c in range(CH):
        expand[c * KP : (c + 1) * KP, :] = near[:, c * LD : (c + 1) * LD].astype(BF16)

    def collect(b, carry):
        rows = []
        for quad in range(4):
            row = pl.multiple_of(b * 512 + quad * 128, 128)
            per_atom = dot(expand[pl.ds(row, 128), :], member[...])
            for c in range(4):
                rows.append(
                    jnp.sum(
                        per_atom[c * KP : (c + 1) * KP, :] * basis_pad[...], axis=0, keepdims=True
                    )
                )
        pot[pl.ds(pl.multiple_of(b * 16, 16), 16), :] = jnp.concatenate(rows, axis=0).astype(BF16)
        return carry

    pot = r["pot"]
    lax.fori_loop(0, CH // 16, collect, 0)
    pot_all = r["pot_all"]
    pot_copies = [send(pot, pot_all.at[mine, :], d) for d in chan_peers]
    pot_all[mine, :] = pot[...]

    for copy in z_copies:
        copy.wait()
    summed = z_in[0].astype(F32)
    for i in range(1, n_z):
        summed = summed + z_in[i].astype(F32)
    total[m] = summed.astype(BF16)
    gather_copies = [send(total.at[m], total.at[m], device) for _, device in plane_peers]

    for copy in pot_copies:
        copy.wait()
    r["refined"][...] = (
        r["charges"][...].astype(F32) + dot(r["mixt"][mine, :], pot_all[...])
    ).astype(BF16)
    for copy in gather_copies:
        copy.wait()


def final_kernel(refined_ref, total_ref, out_ref, gl_ref, gc_ref, rows):
    k, _, slots = gl_ref.shape
    out_ref[...] = refined_ref[...]
    n, rc, _ = total_ref.shape
    for d in range(n):
        rows[d * rc : (d + 1) * rc, :] = total_ref[d].astype(F32)
    for i in range(k):
        block = rows[i * k : (i + 1) * k, :]
        gl_ref[i] = block[:, 0:slots]
        gc_ref[i] = pltpu.roll(block, 128 - slots, 1)[:, 0:slots]


VMEM = pl.BlockSpec(memory_space=pltpu.VMEM)
HBM = pl.BlockSpec(memory_space=pltpu.HBM)


def call(kernel, outs, scratch, args, mib, space, collective=None):
    extra = {}
    if collective is not None:
        extra = dict(collective_id=collective, has_side_effects=True)
    return pl.pallas_call(
        kernel,
        out_shape=outs,
        in_specs=[space] * len(args),
        out_specs=[VMEM] * len(outs),
        scratch_shapes=scratch,
        compiler_params=pltpu.CompilerParams(vmem_limit_bytes=mib << 20, **extra),
    )(*args)


def local(n_cells, n_chan, n_x, n_z, charges, basis, atom_leaf, leaf_lists, coarse_lists, up_ops, down_ops, leaf_ops,
          coarse_ops, mix, cotangent):
    k, atoms = basis.shape
    slots = leaf_lists.shape[0]
    shape = jax.ShapeDtypeStruct
    n_plane = 2 * n_x * n_chan
    rc = -(-k * k // (8 * n_plane)) * 8
    args = dict(
        charges=charges, basis=basis, leaf=atom_leaf.reshape(1, atoms), leaf_lists=leaf_lists,
        coarse_lists=coarse_lists.T, up=jnp.transpose(up_ops, (1, 0, 2)), down=jnp.transpose(down_ops, (1, 0, 2)), leaf_ops=leaf_ops, coarse_ops=coarse_ops,
        mix=mix, cot=cotangent,
    )
    outs = dict(
        refined=shape((CH, atoms), BF16),
        total=shape((n_plane, rc, 128), BF16),
    )
    copies = 2 * (n_chan - 1) + 4 + 2 * (n_plane - 1) + n_z - 1
    scratch = dict(
        cot_all=((n_chan * CH, atoms), BF16),
        basis_pad=((KP, atoms), F32),
        member=((LD, atoms), BF16),
        octants=((1024, 1024), BF16),
        stack=((8 * KP, CH * CD), BF16),
        back_pot=((CH, atoms), BF16),
        src=((CH * KP, 2 * LD), BF16),
        csrc=((4 * KP, 256), BF16),
        bexp=((CH * KP, LD), BF16),
        back=((KP, CH * LD), BF16),
        bfar=((KP, CH * CD), BF16),
        to_left=((512, LD), BF16),
        to_right=((512, LD), BF16),
        from_right=((512, LD), BF16),
        from_left=((512, LD), BF16),
        coarse=((KP, CH * CD), BF16),
        coarse_right=((KP, CH * CD), BF16),
        coarse_left=((KP, CH * CD), BF16),
        up_pad=((8 * KP, KP), F32),
        down_pad=((8 * KP, KP), F32),
        lists=((slots, LD), jnp.int32),
        clists=((slots, 128), jnp.int32),
        picked=((slots * KP, CH * LD), BF16),
        cpicked=((slots * KP, CH * CD), BF16),
        child=((8 * KP, CH * LD), BF16),
        near=((KP, CH * LD), F32),
        up_rows=((8 * k, 128), F32),
        down_rows=((8 * k, 128), F32),
        pot_all=((n_chan * CH, atoms), BF16),
        mixt=(mix.shape, BF16),
        ops_rows=((KP * KP, 128), F32),
        ops_turned=((2 * slots * KP, 128), F32),
        slots=((2 * slots * KP, 128), F32),
        ops=((2 * slots * KP, KP), BF16),
        pot=((CH, atoms), BF16),
        grad=((n_plane * rc, 128), F32),
        grad16=((n_plane, rc, 128), BF16),
        part_in=((n_plane - 1, rc, 128), BF16),
        part=((rc, 128), BF16),
        z_in=((n_z, rc, 128), BF16),
    )
    for name, value in args.items():
        if name != "cot":
            scratch[name] = (value.shape, value.dtype)
    names = tuple(n + "_hbm" for n in ARGS) + tuple(outs) + tuple(scratch) + ("loads", "sends", "recvs")
    refined, total = call(
        functools.partial(main_kernel, n_cells, n_chan, n_x, n_z, rc, names),
        list(outs.values()),
        [pltpu.VMEM(*v) for v in scratch.values()]
        + [pltpu.SemaphoreType.DMA((n,)) for n in (len(args), copies, copies)],
        tuple(args[n] for n in ARGS),
        60,
        HBM,
        collective=0,
    )
    return call(
        final_kernel,
        [shape((CH, atoms), BF16), shape((k, k, slots), F32), shape((k, k, slots), F32)],
        [pltpu.VMEM((n_plane * rc, 128), F32)],
        (refined, total),
        60,
        VMEM,
    )


def solution(mesh):
    n_cells, n_chan = mesh.shape["cells"], mesh.shape["chan"]
    n_x = 4 if n_cells % 8 == 0 and n_cells > 8 else 2
    n_z = n_cells // (2 * n_x)
    placed = (
        P("chan", "cells"),
        P(None, "cells"),
        P("cells"),
        P(None, "cells"),
        P(None, "cells"),
        P(),
        P(),
        P(),
        P(),
        P(),
        P("chan", "cells"),
    )
    return jax.shard_map(
        functools.partial(local, n_cells, n_chan, n_x, n_z),
        mesh=mesh,
        in_specs=placed,
        out_specs=(P("chan", "cells"), P(), P()),
        check_vma=False,
    )
```

```python
import functools

import jax
import jax.numpy as jnp
from jax import lax
from jax.experimental import pallas as pl
from jax.experimental.pallas import tpu as pltpu
from jax.sharding import PartitionSpec as P

MESH = pl.DeviceIdType.MESH
BF16 = jnp.bfloat16
F32 = jnp.float32
ARGS = ("leaf", "basis", "charges", "cot", "up", "down", "leaf_lists", "coarse_lists", "leaf_ops", "coarse_ops", "mix")
KP = 32
CH = 32
LD = 128
CD = 16
SG = 8
NN = (((1,), (0,)), ((), ()))
NT = (((1,), (1,)), ((), ()))
TN = (((0,), (0,)), ((), ()))


def dot(a, b, dims=NN):
    return lax.dot_general(a, b, dims, preferred_element_type=F32)


def one_hot(row, rows):
    index = lax.broadcasted_iota(jnp.int32, (rows, row.shape[1]), 0)
    return jnp.where(index == row, 1.0, 0.0).astype(BF16)


def lane_iota(rows, lanes):
    return lax.broadcasted_iota(jnp.int32, (rows, lanes), 1)


def fill_member(leaf_ref, member, first):
    member[...] = one_hot(leaf_ref[...] - first, LD)


def fill_basis(basis_ref, basis_pad):
    k = basis_ref.shape[0]
    basis_pad[...] = jnp.zeros_like(basis_pad)
    basis_pad[0:k, :] = basis_ref[...]


def fill_octants(octants):
    for o in range(8):
        lane = lane_iota(1, 128)
        row = (lane >> 4) * 128 + 8 * (lane & 15) + o
        octants[:, o * 128 : (o + 1) * 128] = one_hot(row, 1024)


def spread(values_ref, basis_pad, member, out):
    def block(b, carry):
        values = values_ref[pl.ds(pl.multiple_of(b * 16, 16), 16), :].astype(F32)
        for quad in range(4):
            scaled = jnp.concatenate(
                [
                    (basis_pad[...] * values[c : c + 1, :]).astype(BF16)
                    for c in range(quad * 4, quad * 4 + 4)
                ],
                axis=0,
            )
            row = pl.multiple_of(b * 512 + quad * 128, 128)
            out[pl.ds(row, 128), 0:LD] = dot(scaled, member[...], NT).astype(BF16)
        return carry

    lax.fori_loop(0, CH // 16, block, 0)


def to_parents(fields, octants, ops, dims, stack):
    wide = jnp.concatenate(
        [
            jnp.concatenate(
                [fields[(cb * 8 + c) * KP : (cb * 8 + c + 1) * KP, 0:LD] for c in range(8)], axis=1
            )
            for cb in range(4)
        ],
        axis=0,
    )
    for o in range(8):
        part = dot(wide, octants[:, o * 128 : (o + 1) * 128]).astype(BF16)
        for cb in range(4):
            stack[o * KP : (o + 1) * KP, cb * 128 : (cb + 1) * 128] = part[cb * KP : (cb + 1) * KP]
    return dot(ops, stack[...], dims).astype(BF16)


def gather_group(lists, group, source, picked, base):
    rows = lists[pl.ds(pl.multiple_of(group * SG, SG), SG), :]
    blocks = source.shape[0] // KP
    for pair in range(SG // 2):
        hot = jnp.concatenate(
            [one_hot(rows[s : s + 1, :], 256) for s in (2 * pair, 2 * pair + 1)], axis=1
        )
        for part in range(0, blocks, 4):
            got = dot(source[part * KP : (part + 4) * KP, :], hot).astype(BF16)
            for half in range(2):
                s = 2 * pair + half
                for i in range(4):
                    c = part + i
                    picked[pl.ds(base + s * KP, KP), c * 128 : (c + 1) * 128] = got[
                        i * KP : (i + 1) * KP, half * 128 : (half + 1) * 128
                    ]


def group_rows(g):
    return pl.ds(pl.multiple_of(g * SG * KP, SG * KP), SG * KP)


def turn_ops(leaf_ops_ref, coarse_ops_ref, rows, turned, ops):
    k, _, s = leaf_ops_ref.shape
    rows[...] = jnp.zeros_like(rows)
    turned[...] = jnp.zeros_like(turned)
    for i in range(k):
        both = jnp.concatenate([leaf_ops_ref[i].astype(F32), coarse_ops_ref[i].astype(F32)], axis=1)
        rows[i * KP : i * KP + k, :] = both
    for j in range(k):
        turned[pl.ds(j, 2 * s, stride=KP), 0:KP] = rows[pl.ds(j, KP, stride=KP), :].T
    ops[...] = turned[:, 0:KP].astype(BF16)


def main_kernel(n_cells, n_chan, n_x, n_z, rc, names, *refs):
    r = dict(zip(names, refs))
    cells = lax.axis_index("cells")
    chan = lax.axis_index("chan")
    core = lax.rem(cells, 2)
    x = lax.rem(cells // 2, n_x)
    z = cells // (2 * n_x)
    n_plane = 2 * n_x * n_chan
    m = (x * n_chan + chan) * 2 + core
    k = r["basis_hbm"].shape[0]
    n_slots = r["leaf_lists_hbm"].shape[0]
    groups = n_slots // SG
    left = (lax.rem(cells + n_cells - 1, n_cells), chan)
    right = (lax.rem(cells + 1, n_cells), chan)
    chan_peers = [(cells, lax.rem(chan + i, n_chan)) for i in range(1, n_chan)]
    plane_peers, z_peers = [], []
    far_first = sorted(
        range(1, n_plane),
        key=lambda i: -min(i // (2 * n_chan), n_x - i // (2 * n_chan)) - min(i // 2 % n_chan, n_chan - i // 2 % n_chan),
    )
    for i in far_first:
        d = lax.rem(m + i, n_plane)
        place = d // 2
        plane_peers.append(
            (d, ((z * n_x + place // n_chan) * 2 + lax.rem(d, 2), lax.rem(place, n_chan)))
        )
    for i in sorted(range(1, n_z), key=lambda i: -min(i, n_z - i)):
        d = lax.rem(z + i, n_z)
        z_peers.append((d, ((d * n_x + x) * 2 + core, chan)))

    barrier = pltpu.get_barrier_semaphore()
    greeted = chan_peers + [left, right] + [d for _, d in plane_peers] + [d for _, d in z_peers]
    for device in greeted:
        pl.semaphore_signal(barrier, inc=1, device_id=device, device_id_type=MESH)

    pending = {}
    for i, name in enumerate(ARGS):
        if name == "cot":
            target = r["cot_all"].at[pl.ds(pl.multiple_of(chan * CH, CH), CH), :]
        else:
            target = r[name]
        pending[name] = pltpu.make_async_copy(r[name + "_hbm"], target, r["loads"].at[i])
        pending[name].start()

    def load(*names):
        for name in names:
            pending.pop(name).wait()

    sems = {"next": 0}

    def send(source, target, device):
        i = sems["next"]
        sems["next"] = i + 1
        copy = pltpu.make_async_remote_copy(
            src_ref=source,
            dst_ref=target,
            send_sem=r["sends"].at[i],
            recv_sem=r["recvs"].at[i],
            device_id=device,
            device_id_type=MESH,
        )
        copy.start()
        return copy

    member, basis_pad, src, bexp = r["member"], r["basis_pad"], r["src"], r["bexp"]
    load("leaf", "basis")
    fill_member(r["leaf"], member, cells * LD)
    fill_basis(r["basis"], basis_pad)

    load("charges")
    spread(r["charges"], basis_pad, member, src)
    low = lane_iota(512, 128) < 64
    top = src[0:512, 0:LD].astype(F32)
    bottom = pltpu.roll(src[512:1024, 0:LD].astype(F32), 64, 1)
    r["to_left"][...] = jnp.where(low, top, bottom).astype(BF16)
    r["to_right"][...] = jnp.where(low, bottom, top).astype(BF16)

    pl.semaphore_wait(barrier, len(greeted))
    mine = pl.ds(pl.multiple_of(chan * CH, CH), CH)
    halo = [send(r["to_left"], r["from_right"], left), send(r["to_right"], r["from_left"], right)]
    cot_copies = [send(r["cot_hbm"], r["cot_all"].at[mine, :], d) for d in chan_peers]

    load("up", "down")
    for ops_ref, pad, rows in ((r["up"], r["up_pad"], r["up_rows"]), (r["down"], r["down_pad"], r["down_rows"])):
        pad[...] = jnp.zeros_like(pad)
        for i in range(k):
            rows[i * 8 : (i + 1) * 8, 0:k] = ops_ref[i].astype(F32)
        for o in range(8):
            pad[o * KP : o * KP + k, 0:k] = rows[pl.ds(o, k, stride=8), :][:, 0:k]
    fill_octants(r["octants"])

    up_wide = jnp.concatenate([r["up_pad"][o * KP : (o + 1) * KP, :] for o in range(8)], axis=1).astype(BF16)
    down_wide = jnp.concatenate([r["down_pad"][o * KP : (o + 1) * KP, :] for o in range(8)], axis=1).astype(BF16)
    down_tall = r["down_pad"][...].astype(BF16)

    coarse = r["coarse"]
    coarse[...] = to_parents(src, r["octants"], up_wide, NN, r["stack"])
    coarse_halo = [send(coarse, r["coarse_right"], left), send(coarse, r["coarse_left"], right)]

    load("leaf_lists", "coarse_lists", "leaf_ops", "coarse_ops", "mix", "cot")
    raw = r["leaf_lists"][...]
    r["lists"][...] = jnp.where(raw < 0, -1, (raw - cells * LD) & 255)
    raw = r["coarse_lists"][...]
    raw = jnp.concatenate([raw] * 8, axis=0).T
    at = jnp.where(raw < 0, -1, (raw - cells * CD) & 31)
    c8 = (lane_iota(n_slots, 128) >> 4) * CD
    r["clists"][...] = jnp.where(at < 0, -1, jnp.where(at < CD, c8 + at, 112 + c8 + at))


    for copy in halo:
        copy.wait()
    a, b = r["from_right"][...].astype(F32), r["from_left"][...].astype(F32)
    src[0:512, LD : 2 * LD] = jnp.where(low, a, b).astype(BF16)
    src[512:1024, LD : 2 * LD] = pltpu.roll(jnp.where(low, b, a), 64, 1).astype(BF16)
    picked, cpicked, slots = r["picked"], r["cpicked"], r["slots"]

    def leaf_gather(g, carry):
        gather_group(r["lists"], g, src, picked, pl.multiple_of(g * SG * KP, SG * KP))
        return carry

    def leaf_gradient(g, carry):
        slots[group_rows(g), 0:KP] = dot(picked[group_rows(g), :], r["back"][...], NT)
        return carry

    lax.fori_loop(0, 2, leaf_gather, 0)

    for copy in cot_copies:
        copy.wait()
    r["back_pot"][...] = dot(r["mix"][mine, :], r["cot_all"][...]).astype(BF16)
    spread(r["back_pot"], basis_pad, member, bexp)
    for c in range(CH):
        r["back"][:, c * LD : (c + 1) * LD] = bexp[c * KP : (c + 1) * KP, :]
    r["bfar"][...] = to_parents(bexp, r["octants"], down_tall, TN, r["stack"])

    for copy in coarse_halo:
        copy.wait()
    first = (lane_iota(KP, 128) & 15) < 8
    csrc = r["csrc"]
    for cb in range(4):
        lanes = slice(cb * 128, (cb + 1) * 128)
        rows = slice(cb * KP, (cb + 1) * KP)
        csrc[rows, 0:128] = coarse[:, lanes]
        csrc[rows, 128:256] = jnp.where(
            first, r["coarse_right"][:, lanes].astype(F32), r["coarse_left"][:, lanes].astype(F32)
        ).astype(BF16)

    def coarse_group(h, carry):
        for i in range(2):
            g = 2 * h + i
            gather_group(r["clists"], g, csrc, cpicked, pl.multiple_of(g * SG * KP, SG * KP))
        return carry

    lax.fori_loop(0, groups // 2, coarse_group, 0)
    slots[groups * SG * KP : 2 * groups * SG * KP, 0:KP] = dot(cpicked[...], r["bfar"][...], NT)

    def leaf_group(g, carry):
        leaf_gather(g, 0)
        return leaf_gradient(g, 0)

    lax.fori_loop(0, 2, leaf_gradient, 0)
    lax.fori_loop(2, groups, leaf_group, 0)

    grad, grad16, part_in, z_in, total = (r[n] for n in ("grad", "grad16", "part_in", "z_in", "total"))
    used = k * k // 8 * 8
    grad[used:, :] = jnp.zeros((n_plane * rc - used, 128), F32)
    for j in range(k):
        turned = slots[pl.ds(j, 2 * n_slots, stride=KP), :].T
        grad[pl.ds(j, k, stride=k), :] = turned[0:k, :]
    for d in range(n_plane):
        grad16[d] = grad[d * rc : (d + 1) * rc, :].astype(BF16)
    plane_copies = [
        send(grad16.at[d], part_in.at[i], device) for i, (d, device) in enumerate(plane_peers)
    ]

    turn_ops(r["leaf_ops"], r["coarse_ops"], r["ops_rows"], r["ops_turned"], r["ops"])
    r["mixt"][...] = r["mix"][...].astype(F32).T.astype(BF16)
    near = r["near"]
    far16 = dot(r["ops"][groups * SG * KP : 2 * groups * SG * KP, :], cpicked[...], TN).astype(BF16)

    far_rows = jnp.concatenate([far16[:, cb * 128 : (cb + 1) * 128] for cb in range(4)], axis=0)
    octant = lane_iota(KP, 128) & 7
    child = r["child"]
    for c in range(8):
        parent = (lane_iota(1, 128) >> 3) + c * CD
        wide = dot(far_rows, one_hot(parent, 128))
        for cb in range(4):
            lanes = slice((cb * 8 + c) * 128, (cb * 8 + c + 1) * 128)
            block = wide[cb * KP : (cb + 1) * KP, :]
            for o in range(8):
                child[o * KP : (o + 1) * KP, lanes] = jnp.where(octant == o, block, 0.0).astype(BF16)
    for c in range(0, CH * LD, 512):
        near[:, c : c + 512] = dot(down_wide, child[:, c : c + 512])

    def near_group(g, carry):
        ops = r["ops"][group_rows(g), :]
        for c in range(0, CH * LD, 512):
            near[:, c : c + 512] += dot(ops, picked[group_rows(g), c : c + 512], TN)
        return carry

    lax.fori_loop(0, groups // 2, near_group, 0)
    for copy in plane_copies:
        copy.wait()
    summed = grad[pl.ds(pl.multiple_of(m * rc, 8), rc), :]
    for i in range(n_plane - 1):
        summed = summed + part_in[i].astype(F32)
    r["part"][...] = summed.astype(BF16)
    z_copies = [send(r["part"], z_in.at[z], device) for _, device in z_peers]
    z_in[z] = summed.astype(BF16)
    lax.fori_loop(groups // 2, groups, near_group, 0)

    expand = bexp
    for c in range(CH):
        expand[c * KP : (c + 1) * KP, :] = near[:, c * LD : (c + 1) * LD].astype(BF16)

    def collect(b, carry):
        rows = []
        for quad in range(4):
            row = pl.multiple_of(b * 512 + quad * 128, 128)
            per_atom = dot(expand[pl.ds(row, 128), :], member[...])
            for c in range(4):
                rows.append(
                    jnp.sum(
                        per_atom[c * KP : (c + 1) * KP, :] * basis_pad[...], axis=0, keepdims=True
                    )
                )
        pot[pl.ds(pl.multiple_of(b * 16, 16), 16), :] = jnp.concatenate(rows, axis=0).astype(BF16)
        return carry

    pot = r["pot"]
    lax.fori_loop(0, CH // 16, collect, 0)
    pot_all = r["pot_all"]
    pot_copies = [send(pot, pot_all.at[mine, :], d) for d in chan_peers]
    pot_all[mine, :] = pot[...]

    for copy in z_copies:
        copy.wait()
    summed = z_in[0].astype(F32)
    for i in range(1, n_z):
        summed = summed + z_in[i].astype(F32)
    r["own"][...] = summed.astype(BF16)
    gather_copies = [send(r["own"], total.at[m], device) for _, device in plane_peers]
    stores = [pltpu.make_async_copy(r["own"], total.at[m], r["stores"].at[0])]
    stores[0].start()

    for copy in pot_copies:
        copy.wait()
    r["mixed"][...] = (
        r["charges"][...].astype(F32) + dot(r["mixt"][mine, :], pot_all[...])
    ).astype(BF16)
    stores.append(pltpu.make_async_copy(r["mixed"], r["refined"], r["stores"].at[1]))
    stores[1].start()
    for copy in gather_copies + stores:
        copy.wait()


def final_kernel(refined_ref, total_ref, out_ref, gl_ref, gc_ref, rows):
    k, _, slots = gl_ref.shape
    out_ref[...] = refined_ref[...]
    n, rc, _ = total_ref.shape
    for d in range(n):
        rows[d * rc : (d + 1) * rc, :] = total_ref[d].astype(F32)
    for i in range(k):
        block = rows[i * k : (i + 1) * k, :]
        gl_ref[i] = block[:, 0:slots]
        gc_ref[i] = pltpu.roll(block, 128 - slots, 1)[:, 0:slots]


VMEM = pl.BlockSpec(memory_space=pltpu.VMEM)
HBM = pl.BlockSpec(memory_space=pltpu.HBM)


def call(kernel, outs, scratch, args, kib, space, collective=None):
    extra = {}
    if collective is not None:
        extra = dict(collective_id=collective, has_side_effects=True)
    return pl.pallas_call(
        kernel,
        out_shape=outs,
        in_specs=[space] * len(args),
        out_specs=[space if collective is not None else VMEM] * len(outs),
        scratch_shapes=scratch,
        compiler_params=pltpu.CompilerParams(vmem_limit_bytes=kib << 10, **extra),
    )(*args)


def local(n_cells, n_chan, n_x, n_z, charges, basis, atom_leaf, leaf_lists, coarse_lists, up_ops, down_ops, leaf_ops,
          coarse_ops, mix, cotangent):
    k, atoms = basis.shape
    slots = leaf_lists.shape[0]
    shape = jax.ShapeDtypeStruct
    n_plane = 2 * n_x * n_chan
    rc = -(-k * k // (8 * n_plane)) * 8
    args = dict(
        charges=charges, basis=basis, leaf=atom_leaf.reshape(1, atoms), leaf_lists=leaf_lists,
        coarse_lists=coarse_lists.T, up=jnp.transpose(up_ops, (1, 0, 2)), down=jnp.transpose(down_ops, (1, 0, 2)), leaf_ops=leaf_ops, coarse_ops=coarse_ops,
        mix=mix, cot=cotangent,
    )
    outs = dict(
        refined=shape((CH, atoms), BF16),
        total=shape((n_plane, rc, 128), BF16),
    )
    copies = 2 * (n_chan - 1) + 4 + 2 * (n_plane - 1) + n_z - 1
    scratch = dict(
        cot_all=((n_chan * CH, atoms), BF16),
        basis_pad=((KP, atoms), F32),
        member=((LD, atoms), BF16),
        octants=((1024, 1024), BF16),
        stack=((8 * KP, CH * CD), BF16),
        back_pot=((CH, atoms), BF16),
        src=((CH * KP, 2 * LD), BF16),
        csrc=((4 * KP, 256), BF16),
        bexp=((CH * KP, LD), BF16),
        back=((KP, CH * LD), BF16),
        bfar=((KP, CH * CD), BF16),
        to_left=((512, LD), BF16),
        to_right=((512, LD), BF16),
        from_right=((512, LD), BF16),
        from_left=((512, LD), BF16),
        coarse=((KP, CH * CD), BF16),
        coarse_right=((KP, CH * CD), BF16),
        coarse_left=((KP, CH * CD), BF16),
        up_pad=((8 * KP, KP), F32),
        down_pad=((8 * KP, KP), F32),
        lists=((slots, LD), jnp.int32),
        clists=((slots, 128), jnp.int32),
        picked=((slots * KP, CH * LD), BF16),
        cpicked=((slots * KP, CH * CD), BF16),
        child=((8 * KP, CH * LD), BF16),
        near=((KP, CH * LD), F32),
        up_rows=((8 * k, 128), F32),
        down_rows=((8 * k, 128), F32),
        pot_all=((n_chan * CH, atoms), BF16),
        mixt=(mix.shape, BF16),
        ops_rows=((KP * KP, 128), F32),
        ops_turned=((2 * slots * KP, 128), F32),
        slots=((2 * slots * KP, 128), F32),
        ops=((2 * slots * KP, KP), BF16),
        pot=((CH, atoms), BF16),
        grad=((n_plane * rc, 128), F32),
        grad16=((n_plane, rc, 128), BF16),
        part_in=((n_plane - 1, rc, 128), BF16),
        part=((rc, 128), BF16),
        own=((rc, 128), BF16),
        mixed=((CH, atoms), BF16),
        z_in=((n_z, rc, 128), BF16),
    )
    for name, value in args.items():
        if name != "cot":
            scratch[name] = (value.shape, value.dtype)
    names = tuple(n + "_hbm" for n in ARGS) + tuple(outs) + tuple(scratch) + ("loads", "stores", "sends", "recvs")
    refined, total = call(
        functools.partial(main_kernel, n_cells, n_chan, n_x, n_z, rc, names),
        list(outs.values()),
        [pltpu.VMEM(*v) for v in scratch.values()]
        + [pltpu.SemaphoreType.DMA((n,)) for n in (len(args), 2, copies, copies)],
        tuple(args[n] for n in ARGS),
        60 << 10,
        HBM,
        collective=0,
    )
    return call(
        final_kernel,
        [shape((CH, atoms), BF16), shape((k, k, slots), F32), shape((k, k, slots), F32)],
        [pltpu.VMEM((n_plane * rc, 128), F32)],
        (refined, total),
        60 << 10,
        VMEM,
    )


def solution(mesh):
    n_cells, n_chan = mesh.shape["cells"], mesh.shape["chan"]
    n_x = 4 if n_cells % 8 == 0 and n_cells > 8 else 2
    n_z = n_cells // (2 * n_x)
    placed = (
        P("chan", "cells"),
        P(None, "cells"),
        P("cells"),
        P(None, "cells"),
        P(None, "cells"),
        P(),
        P(),
        P(),
        P(),
        P(),
        P("chan", "cells"),
    )
    return jax.shard_map(
        functools.partial(local, n_cells, n_chan, n_x, n_z),
        mesh=mesh,
        in_specs=placed,
        out_specs=(P("chan", "cells"), P(), P()),
        check_vma=False,
    )
```

```python
import functools

import jax
import jax.numpy as jnp
from jax import lax
from jax.experimental import pallas as pl
from jax.experimental.pallas import tpu as pltpu
from jax.sharding import PartitionSpec as P

MESH = pl.DeviceIdType.MESH
BF16 = jnp.bfloat16
F32 = jnp.float32
ARGS = ("leaf", "basis", "charges", "cot", "up", "down", "leaf_lists", "coarse_lists", "leaf_ops", "coarse_ops", "mix")
KP = 32
CH = 32
LD = 128
CD = 16
SG = 8
NN = (((1,), (0,)), ((), ()))
NT = (((1,), (1,)), ((), ()))
TN = (((0,), (0,)), ((), ()))


def dot(a, b, dims=NN):
    return lax.dot_general(a, b, dims, preferred_element_type=F32)


def one_hot(row, rows):
    index = lax.broadcasted_iota(jnp.int32, (rows, row.shape[1]), 0)
    return jnp.where(index == row, 1.0, 0.0).astype(BF16)


def lane_iota(rows, lanes):
    return lax.broadcasted_iota(jnp.int32, (rows, lanes), 1)


def fill_member(leaf_ref, member, first):
    member[...] = one_hot(leaf_ref[...] - first, LD)


def fill_basis(basis_ref, basis_pad):
    k = basis_ref.shape[0]
    basis_pad[...] = jnp.zeros_like(basis_pad)
    basis_pad[0:k, :] = basis_ref[...]


def fill_octants(octants):
    for o in range(8):
        lane = lane_iota(1, 128)
        row = (lane >> 4) * 128 + 8 * (lane & 15) + o
        octants[:, o * 128 : (o + 1) * 128] = one_hot(row, 1024)


def spread(values_ref, basis_pad, member, out):
    def block(b, carry):
        values = values_ref[pl.ds(pl.multiple_of(b * 16, 16), 16), :].astype(F32)
        for quad in range(4):
            scaled = jnp.concatenate(
                [
                    (basis_pad[...] * values[c : c + 1, :]).astype(BF16)
                    for c in range(quad * 4, quad * 4 + 4)
                ],
                axis=0,
            )
            row = pl.multiple_of(b * 512 + quad * 128, 128)
            out[pl.ds(row, 128), 0:LD] = dot(scaled, member[...], NT).astype(BF16)
        return carry

    lax.fori_loop(0, CH // 16, block, 0)


def to_parents(fields, octants, ops, dims, stack):
    wide = jnp.concatenate(
        [
            jnp.concatenate(
                [fields[(cb * 8 + c) * KP : (cb * 8 + c + 1) * KP, 0:LD] for c in range(8)], axis=1
            )
            for cb in range(4)
        ],
        axis=0,
    )
    for o in range(8):
        part = dot(wide, octants[:, o * 128 : (o + 1) * 128]).astype(BF16)
        for cb in range(4):
            stack[o * KP : (o + 1) * KP, cb * 128 : (cb + 1) * 128] = part[cb * KP : (cb + 1) * KP]
    return dot(ops, stack[...], dims).astype(BF16)


def gather_group(lists, group, source, picked, base):
    rows = lists[pl.ds(pl.multiple_of(group * SG, SG), SG), :]
    blocks = source.shape[0] // KP
    for pair in range(SG // 2):
        hot = jnp.concatenate(
            [one_hot(rows[s : s + 1, :], 256) for s in (2 * pair, 2 * pair + 1)], axis=1
        )
        for part in range(0, blocks, 4):
            got = dot(source[part * KP : (part + 4) * KP, :], hot).astype(BF16)
            for half in range(2):
                s = 2 * pair + half
                for i in range(4):
                    c = part + i
                    picked[pl.ds(base + s * KP, KP), c * 128 : (c + 1) * 128] = got[
                        i * KP : (i + 1) * KP, half * 128 : (half + 1) * 128
                    ]


def group_rows(g):
    return pl.ds(pl.multiple_of(g * SG * KP, SG * KP), SG * KP)


def turn_ops(leaf_ops_ref, coarse_ops_ref, rows, turned, ops):
    k, _, s = leaf_ops_ref.shape
    rows[...] = jnp.zeros_like(rows)
    turned[...] = jnp.zeros_like(turned)
    for i in range(k):
        both = jnp.concatenate([leaf_ops_ref[i].astype(F32), coarse_ops_ref[i].astype(F32)], axis=1)
        rows[i * KP : i * KP + k, :] = both
    for j in range(k):
        turned[pl.ds(j, 2 * s, stride=KP), 0:KP] = rows[pl.ds(j, KP, stride=KP), :].T
    ops[...] = turned[:, 0:KP].astype(BF16)


def main_kernel(n_cells, n_chan, n_x, n_z, rc, names, *refs):
    r = dict(zip(names, refs))
    cells = lax.axis_index("cells")
    chan = lax.axis_index("chan")
    core = lax.rem(cells, 2)
    x = lax.rem(cells // 2, n_x)
    z = cells // (2 * n_x)
    n_plane = 2 * n_x * n_chan
    m = (x * n_chan + chan) * 2 + core
    k = r["basis_hbm"].shape[0]
    n_slots = r["leaf_lists_hbm"].shape[0]
    groups = n_slots // SG
    left = (lax.rem(cells + n_cells - 1, n_cells), chan)
    right = (lax.rem(cells + 1, n_cells), chan)
    chan_peers = [
        (cells, lax.rem(chan + i, n_chan)) for i in sorted(range(1, n_chan), key=lambda i: -min(i, n_chan - i))
    ]
    plane_peers, z_peers = [], []
    far_first = sorted(
        range(1, n_plane),
        key=lambda i: -min(i // (2 * n_chan), n_x - i // (2 * n_chan)) - min(i // 2 % n_chan, n_chan - i // 2 % n_chan),
    )
    for i in far_first:
        d = lax.rem(m + i, n_plane)
        place = d // 2
        plane_peers.append(
            (d, ((z * n_x + place // n_chan) * 2 + lax.rem(d, 2), lax.rem(place, n_chan)))
        )
    for i in sorted(range(1, n_z), key=lambda i: -min(i, n_z - i)):
        d = lax.rem(z + i, n_z)
        z_peers.append((d, ((d * n_x + x) * 2 + core, chan)))

    barrier = pltpu.get_barrier_semaphore()
    greeted = chan_peers + [left, right] + [d for _, d in plane_peers] + [d for _, d in z_peers]
    for device in greeted:
        pl.semaphore_signal(barrier, inc=1, device_id=device, device_id_type=MESH)

    pending = {}
    for i, name in enumerate(ARGS):
        if name == "cot":
            target = r["cot_all"].at[pl.ds(pl.multiple_of(chan * CH, CH), CH), :]
        else:
            target = r[name]
        pending[name] = pltpu.make_async_copy(r[name + "_hbm"], target, r["loads"].at[i])
        pending[name].start()

    def load(*names):
        for name in names:
            pending.pop(name).wait()

    sems = {"next": 0}

    def send(source, target, device):
        i = sems["next"]
        sems["next"] = i + 1
        copy = pltpu.make_async_remote_copy(
            src_ref=source,
            dst_ref=target,
            send_sem=r["sends"].at[i],
            recv_sem=r["recvs"].at[i],
            device_id=device,
            device_id_type=MESH,
        )
        copy.start()
        return copy

    member, basis_pad, src, bexp = r["member"], r["basis_pad"], r["src"], r["bexp"]
    load("leaf", "basis")
    fill_member(r["leaf"], member, cells * LD)
    fill_basis(r["basis"], basis_pad)

    load("charges")
    spread(r["charges"], basis_pad, member, src)
    low = lane_iota(512, 128) < 64
    top = src[0:512, 0:LD].astype(F32)
    bottom = pltpu.roll(src[512:1024, 0:LD].astype(F32), 64, 1)
    r["to_left"][...] = jnp.where(low, top, bottom).astype(BF16)
    r["to_right"][...] = jnp.where(low, bottom, top).astype(BF16)

    pl.semaphore_wait(barrier, len(greeted))
    mine = pl.ds(pl.multiple_of(chan * CH, CH), CH)
    halo = [send(r["to_left"], r["from_right"], left), send(r["to_right"], r["from_left"], right)]
    cot_copies = [send(r["cot_hbm"], r["cot_all"].at[mine, :], d) for d in chan_peers]

    load("up", "down")
    for ops_ref, pad, rows in ((r["up"], r["up_pad"], r["up_rows"]), (r["down"], r["down_pad"], r["down_rows"])):
        pad[...] = jnp.zeros_like(pad)
        for i in range(k):
            rows[i * 8 : (i + 1) * 8, 0:k] = ops_ref[i].astype(F32)
        for o in range(8):
            pad[o * KP : o * KP + k, 0:k] = rows[pl.ds(o, k, stride=8), :][:, 0:k]
    fill_octants(r["octants"])

    up_wide = jnp.concatenate([r["up_pad"][o * KP : (o + 1) * KP, :] for o in range(8)], axis=1).astype(BF16)
    down_wide = jnp.concatenate([r["down_pad"][o * KP : (o + 1) * KP, :] for o in range(8)], axis=1).astype(BF16)
    down_tall = r["down_pad"][...].astype(BF16)

    coarse = r["coarse"]
    coarse[...] = to_parents(src, r["octants"], up_wide, NN, r["stack"])
    coarse_halo = [send(coarse, r["coarse_right"], left), send(coarse, r["coarse_left"], right)]

    load("leaf_lists", "coarse_lists", "leaf_ops", "coarse_ops", "mix", "cot")
    raw = r["leaf_lists"][...]
    r["lists"][...] = jnp.where(raw < 0, -1, (raw - cells * LD) & 255)
    raw = r["coarse_lists"][...]
    raw = jnp.concatenate([raw] * 8, axis=0).T
    at = jnp.where(raw < 0, -1, (raw - cells * CD) & 31)
    c8 = (lane_iota(n_slots, 128) >> 4) * CD
    r["clists"][...] = jnp.where(at < 0, -1, jnp.where(at < CD, c8 + at, 112 + c8 + at))


    for copy in halo:
        copy.wait()
    a, b = r["from_right"][...].astype(F32), r["from_left"][...].astype(F32)
    src[0:512, LD : 2 * LD] = jnp.where(low, a, b).astype(BF16)
    src[512:1024, LD : 2 * LD] = pltpu.roll(jnp.where(low, b, a), 64, 1).astype(BF16)
    picked, cpicked, slots = r["picked"], r["cpicked"], r["slots"]

    def leaf_gather(g, carry):
        gather_group(r["lists"], g, src, picked, pl.multiple_of(g * SG * KP, SG * KP))
        return carry

    def leaf_gradient(g, carry):
        slots[group_rows(g), 0:KP] = dot(picked[group_rows(g), :], r["back"][...], NT)
        return carry

    lax.fori_loop(0, 2, leaf_gather, 0)

    for copy in coarse_halo:
        copy.wait()
    first = (lane_iota(KP, 128) & 15) < 8
    csrc = r["csrc"]
    for cb in range(4):
        lanes = slice(cb * 128, (cb + 1) * 128)
        rows = slice(cb * KP, (cb + 1) * KP)
        csrc[rows, 0:128] = coarse[:, lanes]
        csrc[rows, 128:256] = jnp.where(
            first, r["coarse_right"][:, lanes].astype(F32), r["coarse_left"][:, lanes].astype(F32)
        ).astype(BF16)

    def coarse_group(h, carry):
        for i in range(2):
            g = 2 * h + i
            gather_group(r["clists"], g, csrc, cpicked, pl.multiple_of(g * SG * KP, SG * KP))
        return carry

    lax.fori_loop(0, groups // 2, coarse_group, 0)

    for copy in cot_copies:
        copy.wait()
    r["back_pot"][...] = dot(r["mix"][mine, :], r["cot_all"][...]).astype(BF16)
    spread(r["back_pot"], basis_pad, member, bexp)
    for c in range(CH):
        r["back"][:, c * LD : (c + 1) * LD] = bexp[c * KP : (c + 1) * KP, :]
    r["bfar"][...] = to_parents(bexp, r["octants"], down_tall, TN, r["stack"])

    slots[groups * SG * KP : 2 * groups * SG * KP, 0:KP] = dot(cpicked[...], r["bfar"][...], NT)

    def leaf_group(g, carry):
        leaf_gather(g, 0)
        return leaf_gradient(g, 0)

    lax.fori_loop(0, 2, leaf_gradient, 0)
    lax.fori_loop(2, groups, leaf_group, 0)

    grad, grad16, part_in, z_in, total = (r[n] for n in ("grad", "grad16", "part_in", "z_in", "total"))
    used = k * k // 8 * 8
    grad[used:, :] = jnp.zeros((n_plane * rc - used, 128), F32)
    for j in range(k):
        turned = slots[pl.ds(j, 2 * n_slots, stride=KP), :].T
        grad[pl.ds(j, k, stride=k), :] = turned[0:k, :]
    for d in range(n_plane):
        grad16[d] = grad[d * rc : (d + 1) * rc, :].astype(BF16)
    plane_copies = [
        send(grad16.at[d], part_in.at[i], device) for i, (d, device) in enumerate(plane_peers)
    ]

    turn_ops(r["leaf_ops"], r["coarse_ops"], r["ops_rows"], r["ops_turned"], r["ops"])
    r["mixt"][...] = r["mix"][...].astype(F32).T.astype(BF16)
    near = r["near"]
    far16 = dot(r["ops"][groups * SG * KP : 2 * groups * SG * KP, :], cpicked[...], TN).astype(BF16)

    far_rows = jnp.concatenate([far16[:, cb * 128 : (cb + 1) * 128] for cb in range(4)], axis=0)
    octant = lane_iota(KP, 128) & 7
    child = r["child"]
    for c in range(8):
        parent = (lane_iota(1, 128) >> 3) + c * CD
        wide = dot(far_rows, one_hot(parent, 128))
        for cb in range(4):
            lanes = slice((cb * 8 + c) * 128, (cb * 8 + c + 1) * 128)
            block = wide[cb * KP : (cb + 1) * KP, :]
            for o in range(8):
                child[o * KP : (o + 1) * KP, lanes] = jnp.where(octant == o, block, 0.0).astype(BF16)
    for c in range(0, CH * LD, 512):
        near[:, c : c + 512] = dot(down_wide, child[:, c : c + 512])

    def near_group(g, carry):
        ops = r["ops"][group_rows(g), :]
        for c in range(0, CH * LD, 512):
            near[:, c : c + 512] += dot(ops, picked[group_rows(g), c : c + 512], TN)
        return carry

    lax.fori_loop(0, groups // 2, near_group, 0)
    for copy in plane_copies:
        copy.wait()
    summed = grad[pl.ds(pl.multiple_of(m * rc, 8), rc), :]
    for i in range(n_plane - 1):
        summed = summed + part_in[i].astype(F32)
    r["part"][...] = summed.astype(BF16)
    z_copies = [send(r["part"], z_in.at[z], device) for _, device in z_peers]
    z_in[z] = summed.astype(BF16)
    lax.fori_loop(groups // 2, groups, near_group, 0)

    expand = bexp
    for c in range(CH):
        expand[c * KP : (c + 1) * KP, :] = near[:, c * LD : (c + 1) * LD].astype(BF16)

    def collect(b, carry):
        rows = []
        for quad in range(4):
            row = pl.multiple_of(b * 512 + quad * 128, 128)
            per_atom = dot(expand[pl.ds(row, 128), :], member[...])
            for c in range(4):
                rows.append(
                    jnp.sum(
                        per_atom[c * KP : (c + 1) * KP, :] * basis_pad[...], axis=0, keepdims=True
                    )
                )
        pot[pl.ds(pl.multiple_of(b * 16, 16), 16), :] = jnp.concatenate(rows, axis=0).astype(BF16)
        return carry

    pot = r["pot"]
    lax.fori_loop(0, CH // 16, collect, 0)
    pot_all = r["pot_all"]
    pot_copies = [send(pot, pot_all.at[mine, :], d) for d in chan_peers]
    pot_all[mine, :] = pot[...]

    for copy in z_copies:
        copy.wait()
    summed = z_in[0].astype(F32)
    for i in range(1, n_z):
        summed = summed + z_in[i].astype(F32)
    r["own"][...] = summed.astype(BF16)
    gather_copies = [send(r["own"], total.at[m], device) for _, device in plane_peers]
    stores = [pltpu.make_async_copy(r["own"], total.at[m], r["stores"].at[0])]
    stores[0].start()

    for copy in pot_copies:
        copy.wait()
    r["mixed"][...] = (
        r["charges"][...].astype(F32) + dot(r["mixt"][mine, :], pot_all[...])
    ).astype(BF16)
    stores.append(pltpu.make_async_copy(r["mixed"], r["refined"], r["stores"].at[1]))
    stores[1].start()
    for copy in gather_copies + stores:
        copy.wait()


def final_kernel(refined_ref, total_ref, out_ref, gl_ref, gc_ref, rows):
    k, _, slots = gl_ref.shape
    out_ref[...] = refined_ref[...]
    n, rc, _ = total_ref.shape
    for d in range(n):
        rows[d * rc : (d + 1) * rc, :] = total_ref[d].astype(F32)
    for i in range(k):
        block = rows[i * k : (i + 1) * k, :]
        gl_ref[i] = block[:, 0:slots]
        gc_ref[i] = pltpu.roll(block, 128 - slots, 1)[:, 0:slots]


VMEM = pl.BlockSpec(memory_space=pltpu.VMEM)
HBM = pl.BlockSpec(memory_space=pltpu.HBM)


def call(kernel, outs, scratch, args, kib, space, collective=None):
    extra = {}
    if collective is not None:
        extra = dict(collective_id=collective, has_side_effects=True)
    return pl.pallas_call(
        kernel,
        out_shape=outs,
        in_specs=[space] * len(args),
        out_specs=[space if collective is not None else VMEM] * len(outs),
        scratch_shapes=scratch,
        compiler_params=pltpu.CompilerParams(vmem_limit_bytes=kib << 10, **extra),
    )(*args)


def local(n_cells, n_chan, n_x, n_z, charges, basis, atom_leaf, leaf_lists, coarse_lists, up_ops, down_ops, leaf_ops,
          coarse_ops, mix, cotangent):
    k, atoms = basis.shape
    slots = leaf_lists.shape[0]
    shape = jax.ShapeDtypeStruct
    n_plane = 2 * n_x * n_chan
    rc = -(-k * k // (8 * n_plane)) * 8
    args = dict(
        charges=charges, basis=basis, leaf=atom_leaf.reshape(1, atoms), leaf_lists=leaf_lists,
        coarse_lists=coarse_lists.T, up=jnp.transpose(up_ops, (1, 0, 2)), down=jnp.transpose(down_ops, (1, 0, 2)), leaf_ops=leaf_ops, coarse_ops=coarse_ops,
        mix=mix, cot=cotangent,
    )
    outs = dict(
        refined=shape((CH, atoms), BF16),
        total=shape((n_plane, rc, 128), BF16),
    )
    copies = 2 * (n_chan - 1) + 4 + 2 * (n_plane - 1) + n_z - 1
    scratch = dict(
        cot_all=((n_chan * CH, atoms), BF16),
        basis_pad=((KP, atoms), F32),
        member=((LD, atoms), BF16),
        octants=((1024, 1024), BF16),
        stack=((8 * KP, CH * CD), BF16),
        back_pot=((CH, atoms), BF16),
        src=((CH * KP, 2 * LD), BF16),
        csrc=((4 * KP, 256), BF16),
        bexp=((CH * KP, LD), BF16),
        back=((KP, CH * LD), BF16),
        bfar=((KP, CH * CD), BF16),
        to_left=((512, LD), BF16),
        to_right=((512, LD), BF16),
        from_right=((512, LD), BF16),
        from_left=((512, LD), BF16),
        coarse=((KP, CH * CD), BF16),
        coarse_right=((KP, CH * CD), BF16),
        coarse_left=((KP, CH * CD), BF16),
        up_pad=((8 * KP, KP), F32),
        down_pad=((8 * KP, KP), F32),
        lists=((slots, LD), jnp.int32),
        clists=((slots, 128), jnp.int32),
        picked=((slots * KP, CH * LD), BF16),
        cpicked=((slots * KP, CH * CD), BF16),
        child=((8 * KP, CH * LD), BF16),
        near=((KP, CH * LD), F32),
        up_rows=((8 * k, 128), F32),
        down_rows=((8 * k, 128), F32),
        pot_all=((n_chan * CH, atoms), BF16),
        mixt=(mix.shape, BF16),
        ops_rows=((KP * KP, 128), F32),
        ops_turned=((2 * slots * KP, 128), F32),
        slots=((2 * slots * KP, 128), F32),
        ops=((2 * slots * KP, KP), BF16),
        pot=((CH, atoms), BF16),
        grad=((n_plane * rc, 128), F32),
        grad16=((n_plane, rc, 128), BF16),
        part_in=((n_plane - 1, rc, 128), BF16),
        part=((rc, 128), BF16),
        own=((rc, 128), BF16),
        mixed=((CH, atoms), BF16),
        z_in=((n_z, rc, 128), BF16),
    )
    for name, value in args.items():
        if name != "cot":
            scratch[name] = (value.shape, value.dtype)
    names = tuple(n + "_hbm" for n in ARGS) + tuple(outs) + tuple(scratch) + ("loads", "stores", "sends", "recvs")
    refined, total = call(
        functools.partial(main_kernel, n_cells, n_chan, n_x, n_z, rc, names),
        list(outs.values()),
        [pltpu.VMEM(*v) for v in scratch.values()]
        + [pltpu.SemaphoreType.DMA((n,)) for n in (len(args), 2, copies, copies)],
        tuple(args[n] for n in ARGS),
        60 << 10,
        HBM,
        collective=0,
    )
    return call(
        final_kernel,
        [shape((CH, atoms), BF16), shape((k, k, slots), F32), shape((k, k, slots), F32)],
        [pltpu.VMEM((n_plane * rc, 128), F32)],
        (refined, total),
        60 << 10,
        VMEM,
    )


def solution(mesh):
    n_cells, n_chan = mesh.shape["cells"], mesh.shape["chan"]
    n_x = 4 if n_cells % 8 == 0 and n_cells > 8 else 2
    n_z = n_cells // (2 * n_x)
    placed = (
        P("chan", "cells"),
        P(None, "cells"),
        P("cells"),
        P(None, "cells"),
        P(None, "cells"),
        P(),
        P(),
        P(),
        P(),
        P(),
        P("chan", "cells"),
    )
    return jax.shard_map(
        functools.partial(local, n_cells, n_chan, n_x, n_z),
        mesh=mesh,
        in_specs=placed,
        out_specs=(P("chan", "cells"), P(), P()),
        check_vma=False,
    )
```

```python
import functools

import jax
import jax.numpy as jnp
from jax import lax
from jax.experimental import pallas as pl
from jax.experimental.pallas import tpu as pltpu
from jax.sharding import PartitionSpec as P

MESH = pl.DeviceIdType.MESH
BF16 = jnp.bfloat16
F32 = jnp.float32
ARGS = ("leaf", "basis", "charges", "cot", "up", "down", "leaf_lists", "coarse_lists", "leaf_ops", "coarse_ops", "mix")
KP = 32
CH = 32
LD = 128
CD = 16
SG = 8
NN = (((1,), (0,)), ((), ()))
NT = (((1,), (1,)), ((), ()))
TN = (((0,), (0,)), ((), ()))


def dot(a, b, dims=NN):
    return lax.dot_general(a, b, dims, preferred_element_type=F32)


def one_hot(row, rows):
    index = lax.broadcasted_iota(jnp.int32, (rows, row.shape[1]), 0)
    return jnp.where(index == row, 1.0, 0.0).astype(BF16)


def lane_iota(rows, lanes):
    return lax.broadcasted_iota(jnp.int32, (rows, lanes), 1)


def fill_member(leaf_ref, member, first):
    member[...] = one_hot(leaf_ref[...] - first, LD)


def fill_basis(basis_ref, basis_pad):
    k = basis_ref.shape[0]
    basis_pad[...] = jnp.zeros_like(basis_pad)
    basis_pad[0:k, :] = basis_ref[...]


def fill_octants(octants):
    for o in range(8):
        lane = lane_iota(1, 128)
        row = (lane >> 4) * 128 + 8 * (lane & 15) + o
        octants[:, o * 128 : (o + 1) * 128] = one_hot(row, 1024)


def spread(values_ref, basis_pad, member, out):
    def block(b, carry):
        values = values_ref[pl.ds(pl.multiple_of(b * 16, 16), 16), :].astype(F32)
        for quad in range(4):
            scaled = jnp.concatenate(
                [
                    (basis_pad[...] * values[c : c + 1, :]).astype(BF16)
                    for c in range(quad * 4, quad * 4 + 4)
                ],
                axis=0,
            )
            row = pl.multiple_of(b * 512 + quad * 128, 128)
            out[pl.ds(row, 128), 0:LD] = dot(scaled, member[...], NT).astype(BF16)
        return carry

    lax.fori_loop(0, CH // 16, block, 0)


def to_parents(fields, octants, ops, dims, stack):
    wide = jnp.concatenate(
        [
            jnp.concatenate(
                [fields[(cb * 8 + c) * KP : (cb * 8 + c + 1) * KP, 0:LD] for c in range(8)], axis=1
            )
            for cb in range(4)
        ],
        axis=0,
    )
    for o in range(8):
        part = dot(wide, octants[:, o * 128 : (o + 1) * 128]).astype(BF16)
        for cb in range(4):
            stack[o * KP : (o + 1) * KP, cb * 128 : (cb + 1) * 128] = part[cb * KP : (cb + 1) * KP]
    return dot(ops, stack[...], dims).astype(BF16)


def gather_group(lists, group, source, picked, base):
    rows = lists[pl.ds(pl.multiple_of(group * SG, SG), SG), :]
    blocks = source.shape[0] // KP
    for pair in range(SG // 2):
        hot = jnp.concatenate(
            [one_hot(rows[s : s + 1, :], 256) for s in (2 * pair, 2 * pair + 1)], axis=1
        )
        for part in range(0, blocks, 4):
            got = dot(source[part * KP : (part + 4) * KP, :], hot).astype(BF16)
            for half in range(2):
                s = 2 * pair + half
                for i in range(4):
                    c = part + i
                    picked[pl.ds(base + s * KP, KP), c * 128 : (c + 1) * 128] = got[
                        i * KP : (i + 1) * KP, half * 128 : (half + 1) * 128
                    ]


def group_rows(g):
    return pl.ds(pl.multiple_of(g * SG * KP, SG * KP), SG * KP)


def turn_ops(leaf_ops_ref, coarse_ops_ref, rows, turned, ops):
    k, _, s = leaf_ops_ref.shape
    rows[...] = jnp.zeros_like(rows)
    turned[...] = jnp.zeros_like(turned)
    for i in range(k):
        both = jnp.concatenate([leaf_ops_ref[i].astype(F32), coarse_ops_ref[i].astype(F32)], axis=1)
        rows[i * KP : i * KP + k, :] = both
    for j in range(k):
        turned[pl.ds(j, 2 * s, stride=KP), 0:KP] = rows[pl.ds(j, KP, stride=KP), :].T
    ops[...] = turned[:, 0:KP].astype(BF16)


def main_kernel(n_cells, n_chan, n_x, n_z, rc, names, *refs):
    r = dict(zip(names, refs))
    cells = lax.axis_index("cells")
    chan = lax.axis_index("chan")
    core = lax.rem(cells, 2)
    x = lax.rem(cells // 2, n_x)
    z = cells // (2 * n_x)
    n_plane = 2 * n_x * n_chan
    m = (x * n_chan + chan) * 2 + core
    k = r["basis_hbm"].shape[0]
    n_slots = r["leaf_lists_hbm"].shape[0]
    groups = n_slots // SG
    left = (lax.rem(cells + n_cells - 1, n_cells), chan)
    right = (lax.rem(cells + 1, n_cells), chan)
    chan_peers = [(cells, lax.rem(chan + i, n_chan)) for i in range(1, n_chan)]
    plane_peers, z_peers = [], []
    far_first = sorted(
        range(1, n_plane),
        key=lambda i: -min(i // (2 * n_chan), n_x - i // (2 * n_chan)) - min(i // 2 % n_chan, n_chan - i // 2 % n_chan),
    )
    for i in far_first:
        d = lax.rem(m + i, n_plane)
        place = d // 2
        plane_peers.append(
            (d, ((z * n_x + place // n_chan) * 2 + lax.rem(d, 2), lax.rem(place, n_chan)))
        )
    for i in sorted(range(1, n_z), key=lambda i: -min(i, n_z - i)):
        d = lax.rem(z + i, n_z)
        z_peers.append((d, ((d * n_x + x) * 2 + core, chan)))

    barrier = pltpu.get_barrier_semaphore()
    greeted = chan_peers + [left, right] + [d for _, d in plane_peers] + [d for _, d in z_peers]
    for device in greeted:
        pl.semaphore_signal(barrier, inc=1, device_id=device, device_id_type=MESH)

    pending = {}
    for i, name in enumerate(ARGS):
        if name == "cot":
            target = r["cot_all"].at[pl.ds(pl.multiple_of(chan * CH, CH), CH), :]
        else:
            target = r[name]
        pending[name] = pltpu.make_async_copy(r[name + "_hbm"], target, r["loads"].at[i])
        pending[name].start()

    def load(*names):
        for name in names:
            pending.pop(name).wait()

    sems = {"next": 0}

    def send(source, target, device):
        i = sems["next"]
        sems["next"] = i + 1
        copy = pltpu.make_async_remote_copy(
            src_ref=source,
            dst_ref=target,
            send_sem=r["sends"].at[i],
            recv_sem=r["recvs"].at[i],
            device_id=device,
            device_id_type=MESH,
        )
        copy.start()
        return copy

    member, basis_pad, src, bexp = r["member"], r["basis_pad"], r["src"], r["bexp"]
    load("leaf", "basis")
    fill_member(r["leaf"], member, cells * LD)
    fill_basis(r["basis"], basis_pad)

    load("charges")
    spread(r["charges"], basis_pad, member, src)
    low = lane_iota(512, 128) < 64
    top = src[0:512, 0:LD].astype(F32)
    bottom = pltpu.roll(src[512:1024, 0:LD].astype(F32), 64, 1)
    r["to_left"][...] = jnp.where(low, top, bottom).astype(BF16)
    r["to_right"][...] = jnp.where(low, bottom, top).astype(BF16)

    fill_octants(r["octants"])
    pl.semaphore_wait(barrier, len(greeted))
    mine = pl.ds(pl.multiple_of(chan * CH, CH), CH)
    halo = [send(r["to_left"], r["from_right"], left), send(r["to_right"], r["from_left"], right)]
    cot_copies = [send(r["cot_hbm"], r["cot_all"].at[mine, :], d) for d in chan_peers]

    load("up", "down")
    for ops_ref, pad, rows in ((r["up"], r["up_pad"], r["up_rows"]), (r["down"], r["down_pad"], r["down_rows"])):
        pad[...] = jnp.zeros_like(pad)
        for i in range(k):
            rows[i * 8 : (i + 1) * 8, 0:k] = ops_ref[i].astype(F32)
        for o in range(8):
            pad[o * KP : o * KP + k, 0:k] = rows[pl.ds(o, k, stride=8), :][:, 0:k]

    up_wide = jnp.concatenate([r["up_pad"][o * KP : (o + 1) * KP, :] for o in range(8)], axis=1).astype(BF16)
    down_wide = jnp.concatenate([r["down_pad"][o * KP : (o + 1) * KP, :] for o in range(8)], axis=1).astype(BF16)
    down_tall = r["down_pad"][...].astype(BF16)

    coarse = r["coarse"]
    coarse[...] = to_parents(src, r["octants"], up_wide, NN, r["stack"])
    coarse_halo = [send(coarse, r["coarse_right"], left), send(coarse, r["coarse_left"], right)]

    load("leaf_lists", "coarse_lists", "leaf_ops", "coarse_ops", "mix", "cot")
    raw = r["leaf_lists"][...]
    r["lists"][...] = jnp.where(raw < 0, -1, (raw - cells * LD) & 255)
    raw = r["coarse_lists"][...]
    raw = jnp.concatenate([raw] * 8, axis=0).T
    at = jnp.where(raw < 0, -1, (raw - cells * CD) & 31)
    c8 = (lane_iota(n_slots, 128) >> 4) * CD
    r["clists"][...] = jnp.where(at < 0, -1, jnp.where(at < CD, c8 + at, 112 + c8 + at))


    for copy in halo:
        copy.wait()
    a, b = r["from_right"][...].astype(F32), r["from_left"][...].astype(F32)
    src[0:512, LD : 2 * LD] = jnp.where(low, a, b).astype(BF16)
    src[512:1024, LD : 2 * LD] = pltpu.roll(jnp.where(low, b, a), 64, 1).astype(BF16)
    picked, cpicked, slots = r["picked"], r["cpicked"], r["slots"]

    def leaf_gather(g, carry):
        gather_group(r["lists"], g, src, picked, pl.multiple_of(g * SG * KP, SG * KP))
        return carry

    def leaf_gradient(g, carry):
        slots[group_rows(g), 0:KP] = dot(picked[group_rows(g), :], r["back"][...], NT)
        return carry

    lax.fori_loop(0, 2, leaf_gather, 0)

    for copy in cot_copies:
        copy.wait()
    r["back_pot"][...] = dot(r["mix"][mine, :], r["cot_all"][...]).astype(BF16)
    spread(r["back_pot"], basis_pad, member, bexp)
    for c in range(CH):
        r["back"][:, c * LD : (c + 1) * LD] = bexp[c * KP : (c + 1) * KP, :]
    r["bfar"][...] = to_parents(bexp, r["octants"], down_tall, TN, r["stack"])

    for copy in coarse_halo:
        copy.wait()
    first = (lane_iota(KP, 128) & 15) < 8
    csrc = r["csrc"]
    for cb in range(4):
        lanes = slice(cb * 128, (cb + 1) * 128)
        rows = slice(cb * KP, (cb + 1) * KP)
        csrc[rows, 0:128] = coarse[:, lanes]
        csrc[rows, 128:256] = jnp.where(
            first, r["coarse_right"][:, lanes].astype(F32), r["coarse_left"][:, lanes].astype(F32)
        ).astype(BF16)

    def coarse_group(h, carry):
        for i in range(2):
            g = 2 * h + i
            gather_group(r["clists"], g, csrc, cpicked, pl.multiple_of(g * SG * KP, SG * KP))
        return carry

    lax.fori_loop(0, groups // 2, coarse_group, 0)
    slots[groups * SG * KP : 2 * groups * SG * KP, 0:KP] = dot(cpicked[...], r["bfar"][...], NT)

    def leaf_group(g, carry):
        leaf_gather(g, 0)
        return leaf_gradient(g, 0)

    lax.fori_loop(0, 2, leaf_gradient, 0)
    lax.fori_loop(2, groups, leaf_group, 0)

    grad, grad16, part_in, z_in, total = (r[n] for n in ("grad", "grad16", "part_in", "z_in", "total"))
    used = k * k // 8 * 8
    grad[used:, :] = jnp.zeros((n_plane * rc - used, 128), F32)
    for j in range(k):
        turned = slots[pl.ds(j, 2 * n_slots, stride=KP), :].T
        grad[pl.ds(j, k, stride=k), :] = turned[0:k, :]
    for d in range(n_plane):
        grad16[d] = grad[d * rc : (d + 1) * rc, :].astype(BF16)
    plane_copies = [
        send(grad16.at[d], part_in.at[i], device) for i, (d, device) in enumerate(plane_peers)
    ]

    turn_ops(r["leaf_ops"], r["coarse_ops"], r["ops_rows"], r["ops_turned"], r["ops"])
    r["mixt"][...] = r["mix"][...].astype(F32).T.astype(BF16)
    near = r["near"]
    far16 = dot(r["ops"][groups * SG * KP : 2 * groups * SG * KP, :], cpicked[...], TN).astype(BF16)

    far_rows = jnp.concatenate([far16[:, cb * 128 : (cb + 1) * 128] for cb in range(4)], axis=0)
    octant = lane_iota(KP, 128) & 7
    child = r["child"]
    for c in range(8):
        parent = (lane_iota(1, 128) >> 3) + c * CD
        wide = dot(far_rows, one_hot(parent, 128))
        for cb in range(4):
            lanes = slice((cb * 8 + c) * 128, (cb * 8 + c + 1) * 128)
            block = wide[cb * KP : (cb + 1) * KP, :]
            for o in range(8):
                child[o * KP : (o + 1) * KP, lanes] = jnp.where(octant == o, block, 0.0).astype(BF16)
    for c in range(0, CH * LD, 512):
        near[:, c : c + 512] = dot(down_wide, child[:, c : c + 512])

    def near_group(g, carry):
        ops = r["ops"][group_rows(g), :]
        for c in range(0, CH * LD, 512):
            near[:, c : c + 512] += dot(ops, picked[group_rows(g), c : c + 512], TN)
        return carry

    lax.fori_loop(0, groups // 2, near_group, 0)
    for copy in plane_copies:
        copy.wait()
    summed = grad[pl.ds(pl.multiple_of(m * rc, 8), rc), :]
    for i in range(n_plane - 1):
        summed = summed + part_in[i].astype(F32)
    r["part"][...] = summed.astype(BF16)
    z_copies = [send(r["part"], z_in.at[z], device) for _, device in z_peers]
    z_in[z] = summed.astype(BF16)
    lax.fori_loop(groups // 2, groups, near_group, 0)

    expand = bexp
    for c in range(CH):
        expand[c * KP : (c + 1) * KP, :] = near[:, c * LD : (c + 1) * LD].astype(BF16)

    def collect(b, carry):
        rows = []
        for quad in range(4):
            row = pl.multiple_of(b * 512 + quad * 128, 128)
            per_atom = dot(expand[pl.ds(row, 128), :], member[...])
            for c in range(4):
                rows.append(
                    jnp.sum(
                        per_atom[c * KP : (c + 1) * KP, :] * basis_pad[...], axis=0, keepdims=True
                    )
                )
        pot[pl.ds(pl.multiple_of(b * 16, 16), 16), :] = jnp.concatenate(rows, axis=0).astype(BF16)
        return carry

    pot = r["pot"]
    lax.fori_loop(0, CH // 16, collect, 0)
    pot_all = r["pot_all"]
    pot_copies = [send(pot, pot_all.at[mine, :], d) for d in chan_peers]
    pot_all[mine, :] = pot[...]

    for copy in z_copies:
        copy.wait()
    summed = z_in[0].astype(F32)
    for i in range(1, n_z):
        summed = summed + z_in[i].astype(F32)
    r["own"][...] = summed.astype(BF16)
    gather_copies = [send(r["own"], total.at[m], device) for _, device in plane_peers]
    stores = [pltpu.make_async_copy(r["own"], total.at[m], r["stores"].at[0])]
    stores[0].start()

    for copy in pot_copies:
        copy.wait()
    r["mixed"][...] = (
        r["charges"][...].astype(F32) + dot(r["mixt"][mine, :], pot_all[...])
    ).astype(BF16)
    stores.append(pltpu.make_async_copy(r["mixed"], r["refined"], r["stores"].at[1]))
    stores[1].start()
    for copy in gather_copies + stores:
        copy.wait()


def final_kernel(refined_ref, total_ref, out_ref, gl_ref, gc_ref, rows):
    k, _, slots = gl_ref.shape
    out_ref[...] = refined_ref[...]
    n, rc, _ = total_ref.shape
    for d in range(n):
        rows[d * rc : (d + 1) * rc, :] = total_ref[d].astype(F32)
    for i in range(k):
        block = rows[i * k : (i + 1) * k, :]
        gl_ref[i] = block[:, 0:slots]
        gc_ref[i] = pltpu.roll(block, 128 - slots, 1)[:, 0:slots]


VMEM = pl.BlockSpec(memory_space=pltpu.VMEM)
HBM = pl.BlockSpec(memory_space=pltpu.HBM)


def call(kernel, outs, scratch, args, kib, space, collective=None):
    extra = {}
    if collective is not None:
        extra = dict(collective_id=collective, has_side_effects=True)
    return pl.pallas_call(
        kernel,
        out_shape=outs,
        in_specs=[space] * len(args),
        out_specs=[space if collective is not None else VMEM] * len(outs),
        scratch_shapes=scratch,
        compiler_params=pltpu.CompilerParams(vmem_limit_bytes=kib << 10, **extra),
    )(*args)


def local(n_cells, n_chan, n_x, n_z, charges, basis, atom_leaf, leaf_lists, coarse_lists, up_ops, down_ops, leaf_ops,
          coarse_ops, mix, cotangent):
    k, atoms = basis.shape
    slots = leaf_lists.shape[0]
    shape = jax.ShapeDtypeStruct
    n_plane = 2 * n_x * n_chan
    rc = -(-k * k // (8 * n_plane)) * 8
    args = dict(
        charges=charges, basis=basis, leaf=atom_leaf.reshape(1, atoms), leaf_lists=leaf_lists,
        coarse_lists=coarse_lists.T, up=jnp.transpose(up_ops, (1, 0, 2)), down=jnp.transpose(down_ops, (1, 0, 2)), leaf_ops=leaf_ops, coarse_ops=coarse_ops,
        mix=mix, cot=cotangent,
    )
    outs = dict(
        refined=shape((CH, atoms), BF16),
        total=shape((n_plane, rc, 128), BF16),
    )
    copies = 2 * (n_chan - 1) + 4 + 2 * (n_plane - 1) + n_z - 1
    scratch = dict(
        cot_all=((n_chan * CH, atoms), BF16),
        basis_pad=((KP, atoms), F32),
        member=((LD, atoms), BF16),
        octants=((1024, 1024), BF16),
        stack=((8 * KP, CH * CD), BF16),
        back_pot=((CH, atoms), BF16),
        src=((CH * KP, 2 * LD), BF16),
        csrc=((4 * KP, 256), BF16),
        bexp=((CH * KP, LD), BF16),
        back=((KP, CH * LD), BF16),
        bfar=((KP, CH * CD), BF16),
        to_left=((512, LD), BF16),
        to_right=((512, LD), BF16),
        from_right=((512, LD), BF16),
        from_left=((512, LD), BF16),
        coarse=((KP, CH * CD), BF16),
        coarse_right=((KP, CH * CD), BF16),
        coarse_left=((KP, CH * CD), BF16),
        up_pad=((8 * KP, KP), F32),
        down_pad=((8 * KP, KP), F32),
        lists=((slots, LD), jnp.int32),
        clists=((slots, 128), jnp.int32),
        picked=((slots * KP, CH * LD), BF16),
        cpicked=((slots * KP, CH * CD), BF16),
        child=((8 * KP, CH * LD), BF16),
        near=((KP, CH * LD), F32),
        up_rows=((8 * k, 128), F32),
        down_rows=((8 * k, 128), F32),
        pot_all=((n_chan * CH, atoms), BF16),
        mixt=(mix.shape, BF16),
        ops_rows=((KP * KP, 128), F32),
        ops_turned=((2 * slots * KP, 128), F32),
        slots=((2 * slots * KP, 128), F32),
        ops=((2 * slots * KP, KP), BF16),
        pot=((CH, atoms), BF16),
        grad=((n_plane * rc, 128), F32),
        grad16=((n_plane, rc, 128), BF16),
        part_in=((n_plane - 1, rc, 128), BF16),
        part=((rc, 128), BF16),
        own=((rc, 128), BF16),
        mixed=((CH, atoms), BF16),
        z_in=((n_z, rc, 128), BF16),
    )
    for name, value in args.items():
        if name != "cot":
            scratch[name] = (value.shape, value.dtype)
    names = tuple(n + "_hbm" for n in ARGS) + tuple(outs) + tuple(scratch) + ("loads", "stores", "sends", "recvs")
    refined, total = call(
        functools.partial(main_kernel, n_cells, n_chan, n_x, n_z, rc, names),
        list(outs.values()),
        [pltpu.VMEM(*v) for v in scratch.values()]
        + [pltpu.SemaphoreType.DMA((n,)) for n in (len(args), 2, copies, copies)],
        tuple(args[n] for n in ARGS),
        60 << 10,
        HBM,
        collective=0,
    )
    return call(
        final_kernel,
        [shape((CH, atoms), BF16), shape((k, k, slots), F32), shape((k, k, slots), F32)],
        [pltpu.VMEM((n_plane * rc, 128), F32)],
        (refined, total),
        60 << 10,
        VMEM,
    )


def solution(mesh):
    n_cells, n_chan = mesh.shape["cells"], mesh.shape["chan"]
    n_x = 4 if n_cells % 8 == 0 and n_cells > 8 else 2
    n_z = n_cells // (2 * n_x)
    placed = (
        P("chan", "cells"),
        P(None, "cells"),
        P("cells"),
        P(None, "cells"),
        P(None, "cells"),
        P(),
        P(),
        P(),
        P(),
        P(),
        P("chan", "cells"),
    )
    return jax.shard_map(
        functools.partial(local, n_cells, n_chan, n_x, n_z),
        mesh=mesh,
        in_specs=placed,
        out_specs=(P("chan", "cells"), P(), P()),
        check_vma=False,
    )
```
